512 devices in a mesh: dp: 16 (over y, x), seq: 32 (over z, core).
Axes of the slice: x: 4, y: 4, z: 16, core: 2. Of those that a mesh axis runs over, the one named last changes fastest.
Arguments:
- tokens: bfloat16 [16, 8192, 4096], P('dp', 'seq'), may hold values from -6 to 6
- w_qkv: bfloat16 [4096, 768], P('dp'), may hold values from -0.09375 to 0.09375
- norm_gain: float32 [256], replicated, may hold values from 0.1 to 1.9
- w_out: bfloat16 [256, 4096], P(None, 'dp'), may hold values from -0.375 to 0.375
Outputs:
- mixed: bfloat16 [16, 8192, 4096], P('dp', 'seq')
The draws below stay inside these ranges and needn't reach their ends.
All inputs are finite; a program needn't handle non-finite values.
Results may differ from the reference program's by a relative error of at most 0.015.
Values may be sent and summed in bfloat16 or wider, within the bound.
A program may use at most 64 MiB of HBM per device.

```python
import jax
import jax.numpy as jnp
from jax import lax

D = 4096
HEAD = 128
HEADS = 2
TOK_DEV = 256
HD = 256
LEN = 8192
BATCH = 16
N_SEQ = 32


def steps_of(stream_key, shape, shards, low, largest):
    loudness = 1.0
    for axis_at, shards_of in shards:
        draws = jax.random.uniform(jax.random.fold_in(jax.random.fold_in(stream_key, 6), axis_at), (shards_of,), jnp.float32, low / len(shards), largest / len(shards))
        loudness = loudness * jnp.repeat(jnp.exp(draws), shape[axis_at] // shards_of).reshape((-1,) + (1,) * (len(shape) - 1 - axis_at))
    return loudness


def bell_draw(key, extent, scale, bound, split=(), kind=jnp.bfloat16):
    gain = steps_of(key, extent, split, -0.22, 0.18) if split else 1.0
    result = jax.random.normal(key, extent, jnp.float32) * scale * gain
    return jnp.minimum(jnp.maximum(result, -bound), bound).astype(kind)


def setup_inputs(seed: int = 0) -> dict:
    key_of = jax.random.split(jax.random.key(seed), 5)
    return {
        "tokens": bell_draw(key_of[0], (BATCH, LEN, D), 1.0, 6.0, ((0, 16), (1, 32))),
        "w_qkv": bell_draw(key_of[1], (D, 3 * HD), D ** -0.5, 0.09375, ((0, 16),)),
        "norm_gain": jnp.clip(1.0 + 0.18 * jax.random.normal(key_of[2], (HD,), jnp.float32), 0.1, 1.9),
        "w_out": bell_draw(key_of[3], (HD, D), HD ** -0.5, 0.375, ((1, 16),)),
    }


def one_sequence(x, w_qkv, norm_gain, w_out):
    proj = jnp.dot(x, w_qkv, preferred_element_type=jnp.float32)
    query = jax.nn.silu(proj[:, :HD]).astype(jnp.bfloat16)
    keys = jax.nn.silu(proj[:, HD:2 * HD]).astype(jnp.bfloat16)
    values = proj[:, 2 * HD:].astype(jnp.bfloat16)
    shape4 = (N_SEQ, TOK_DEV, HEADS, HEAD)
    qf = query.reshape(shape4).astype(jnp.float32)
    kf = keys.reshape(shape4).astype(jnp.float32)
    vf = values.reshape(shape4).astype(jnp.float32)
    state = jnp.einsum('cthA,cthB->chAB', kf, vf)
    running = jnp.cumsum(state, axis=0)
    prefix = jnp.concatenate([jnp.zeros_like(state[:1]), running[:-1]], axis=0)
    prefix = prefix.astype(jnp.bfloat16).astype(jnp.float32)
    inter = jnp.einsum('cthA,chAB->cthB', qf, prefix)
    scores = jnp.einsum('cthA,cshA->chts', qf, kf)
    rows = jnp.arange(TOK_DEV)
    causal = rows[:, None] >= rows[None, :]
    scores = jnp.where(causal[None, None], scores, 0.0).astype(jnp.bfloat16).astype(jnp.float32)
    intra = jnp.einsum('chts,cshB->cthB', scores, vf)
    attended = inter + intra
    meansq = lax.optimization_barrier(jnp.mean(attended * attended, axis=-1, keepdims=True))
    normed = attended * lax.rsqrt(meansq + 1e-06) * norm_gain.reshape(HEADS, HEAD)
    normed = normed.astype(jnp.bfloat16).reshape(LEN, HD)
    return jnp.dot(normed, w_out, preferred_element_type=jnp.float32).astype(jnp.bfloat16)

def reference(tokens, w_qkv, norm_gain, w_out):
    return lax.map(lambda x: one_sequence(x, w_qkv, norm_gain, w_out), tokens)
```

```python
import functools

import jax
import jax.numpy as jnp
from jax import lax
from jax.experimental import pallas as pl
from jax.experimental.pallas import tpu as pltpu
from jax.sharding import PartitionSpec as P

MESH = pl.DeviceIdType.MESH
BF16, F32 = jnp.bfloat16, jnp.float32
HEAD = 128
SIDE = 4
GROUP = 4
GROUPS = 4
TOK = 256
BLK = 256


def mod4(value):
    return lax.rem(value + 8, 4)


def kernel(
    tok_ref, w_ref, gain_ref, wo_ref, out_ref,
    x_buf, kv, q, wo, k_act, v_act, intra, near, far, total, nrm, nrm_out, out_buf,
    kv_acc, q_act, state,
    load_sem, send_sem, full_sem, half_sem, scan_send, near_sem, far_sem, pair_send, pair_recv, store_sem,
):
    dp, seq = lax.axis_index("dp"), lax.axis_index("seq")
    y, x = lax.div(dp, SIDE), lax.rem(dp, SIDE)
    z, core = lax.div(seq, 2), lax.rem(seq, 2)
    grp, mem = lax.div(z, GROUP), lax.rem(z, GROUP)
    sibling = (dp, z * 2 + (1 - core))
    lane = pl.multiple_of(core * HEAD, HEAD)

    def at_xy(axis, off):
        if axis == 0:
            return (y * SIDE + mod4(x + off), seq)
        return (mod4(y + off) * SIDE + x, seq)

    def at_z(g, m):
        return (dp, (g * GROUP + m) * 2 + core)

    loads = [
        pltpu.make_async_copy(w_ref.at[:, pl.ds(2 * HEAD + lane, HEAD)], kv.at[dp, :, pl.ds(0, HEAD)], load_sem.at[0]),
        pltpu.make_async_copy(w_ref.at[:, pl.ds(4 * HEAD + lane, HEAD)], kv.at[dp, :, pl.ds(HEAD, HEAD)], load_sem.at[1]),
        pltpu.make_async_copy(w_ref.at[:, pl.ds(lane, HEAD)], q.at[dp], load_sem.at[2]),
        pltpu.make_async_copy(wo_ref.at[pl.ds(lane, HEAD)], wo.at[dp, pl.ds(lane, HEAD)], load_sem.at[3]),
        pltpu.make_async_copy(tok_ref, x_buf.at[pl.ds(pl.multiple_of(core * TOK, TOK), TOK)], load_sem.at[4]),
    ]
    for copy in loads:
        copy.start()
    far[...] = jnp.zeros_like(far)

    barrier = pltpu.get_barrier_semaphore()
    partners = [sibling]
    for off in (1, 2, 3):
        partners += [at_xy(0, off), at_xy(1, off), at_z(grp, mod4(mem + off)), at_z(mod4(grp + off), mem)]
    for partner in partners:
        pl.semaphore_signal(barrier, inc=1, device_id=partner, device_id_type=MESH)
    pl.semaphore_wait(barrier, len(partners))

    def piece(s, block, half, sub=None):
        rows = BLK // 2 if s < 2 else HEAD // 2
        start = half * rows
        if s == 2:
            start = start + lane
        if sub is not None:
            start, rows = start + sub * (rows // 2), rows // 2
        start = pl.multiple_of(start, 32) if not isinstance(start, int) else start
        return (kv, q, wo)[s].at[block, pl.ds(start, rows)]

    def block_at(half, first, second):
        dy, dx = (second, first) if half == 0 else (first, second)
        return mod4(y + dy) * SIDE + mod4(x + dx)

    def send_full(s, half, block, axis, off):
        ref = piece(s, block, half)
        pltpu.make_async_remote_copy(
            src_ref=ref, dst_ref=ref, send_sem=send_sem.at[s], recv_sem=full_sem.at[s, half, block],
            device_id=at_xy(axis, off), device_id_type=MESH,
        ).start()

    def wait_full(s, half, block):
        ref = piece(s, block, half)
        pltpu.make_async_copy(ref, ref, full_sem.at[s, half, block]).wait()

    def send_half(s, half, block, sub, axis, off):
        ref = piece(s, block, half, sub)
        pltpu.make_async_remote_copy(
            src_ref=ref, dst_ref=ref, send_sem=send_sem.at[s], recv_sem=half_sem.at[s, half, block, sub],
            device_id=at_xy(axis, off), device_id_type=MESH,
        ).start()

    def wait_half(s, half, block, sub):
        ref = piece(s, block, half, sub)
        pltpu.make_async_copy(ref, ref, half_sem.at[s, half, block, sub]).wait()

    def stage0(s):
        for half in (0, 1):
            for off in (1, -1):
                send_full(s, half, dp, half, off)
        for half in (0, 1):
            send_full(s, half, dp, half, 2)
        for half in (0, 1):
            for off in (1, -1):
                send_full(s, half, dp, 1 - half, off)

    def stage1(s):
        for first in (1, -1, 2):
            for half in (0, 1):
                block = block_at(half, first, 0)
                wait_full(s, half, block)
                for off in (1, -1):
                    send_full(s, half, block, 1 - half, off)

    def stage2(s):
        for first in (0, 1, -1, 2):
            for second in (-1, 1):
                for half in (0, 1):
                    block = block_at(half, first, second)
                    wait_full(s, half, block)
                    send_half(s, half, block, 0 if second == -1 else 1, 1 - half, -second)

    def stage3(s):
        for first in (0, 1, -1, 2):
            for half in (0, 1):
                for sub in (0, 1):
                    wait_half(s, half, block_at(half, first, 2), sub)

    def sent(s):
        ref = (kv.at[pl.ds(0, 15)], q.at[pl.ds(0, 15)], wo.at[pl.ds(0, 15), pl.ds(0, HEAD)])[s]
        pltpu.make_async_copy(ref, ref, send_sem.at[s]).wait()

    loads[0].wait()
    loads[1].wait()
    stage0(0)
    tokens_out = pltpu.make_async_remote_copy(
        src_ref=tok_ref, dst_ref=x_buf.at[pl.ds(pl.multiple_of(core * TOK, TOK), TOK)],
        send_sem=pair_send.at[0], recv_sem=pair_recv.at[0], device_id=sibling, device_id_type=MESH,
    )
    tokens_out.start()
    stage1(0)
    loads[2].wait()
    stage0(1)
    stage2(0)
    stage1(1)
    loads[3].wait()
    stage0(2)
    loads[4].wait()
    tokens_out.wait()
    stage3(0)

    def project(weights, acc):
        wide = weights.shape[-1]
        for part in range(4):
            term = jnp.dot(
                x_buf[:, pl.ds(part * 1024, 1024)],
                weights[pl.ds(part * 4, 4)].reshape(1024, wide),
                preferred_element_type=F32,
            )
            if part == 0:
                acc[...] = term
            else:
                acc[...] += term

    project(kv, kv_acc)
    keys_in = kv_acc[:, :HEAD]
    k_act[...] = (keys_in / (1.0 + jnp.exp(-keys_in))).astype(BF16)
    v_act[...] = kv_acc[:, HEAD:].astype(BF16)
    for b in (0, 1):
        rows = pl.ds(b * TOK, TOK)
        state[b] = lax.dot_general(
            k_act[rows], v_act[rows], (((0,), (0,)), ((), ())), preferred_element_type=F32
        )
    near[mem] = (state[0] + state[1]).astype(BF16)

    for off in (1, 2, 3):
        pltpu.make_async_remote_copy(
            src_ref=near.at[mem], dst_ref=near.at[mem], send_sem=scan_send.at[off - 1], recv_sem=near_sem.at[mem],
            device_id=at_z(grp, mod4(mem + off)), device_id_type=MESH,
        ).start()
    stage2(1)
    stage1(2)
    for off in (1, 2, 3):
        m = mod4(mem + off)
        pltpu.make_async_copy(near.at[m], near.at[m], near_sem.at[m]).wait()
    all_near = [near[m].astype(F32) for m in range(GROUP)]
    total[...] = (all_near[0] + all_near[1] + all_near[2] + all_near[3]).astype(BF16)

    for off in (2, 1, 3):
        g = grp + off

        @pl.when(g < GROUPS)
        def _():
            pltpu.make_async_remote_copy(
                src_ref=total, dst_ref=far.at[grp], send_sem=scan_send.at[2 + off], recv_sem=far_sem.at[grp],
                device_id=at_z(g, mem), device_id_type=MESH,
            ).start()

    prefix = jnp.zeros((HEAD, HEAD), F32)
    for m in range(GROUP - 1):
        prefix = prefix + jnp.where(m < mem, all_near[m], 0.0)

    stage2(2)
    stage3(1)
    project(q, q_act)
    queries = q_act[...]
    q_act[...] = queries / (1.0 + jnp.exp(-queries))
    causal = lax.broadcasted_iota(jnp.int32, (TOK, TOK), 0) >= lax.broadcasted_iota(jnp.int32, (TOK, TOK), 1)
    for b in (0, 1):
        rows = pl.ds(b * TOK, TOK)
        scores = lax.dot_general(
            q_act[rows].astype(BF16), k_act[rows], (((1,), (1,)), ((), ())), preferred_element_type=F32
        )
        scores = jnp.where(causal, scores, 0.0).astype(BF16)
        intra[rows] = jnp.dot(scores, v_act[rows], preferred_element_type=F32)
    stage3(2)
    wo_out = pltpu.make_async_remote_copy(
        src_ref=wo.at[:, pl.ds(lane, HEAD)], dst_ref=wo.at[:, pl.ds(lane, HEAD)],
        send_sem=pair_send.at[1], recv_sem=pair_recv.at[1], device_id=sibling, device_id_type=MESH,
    )
    wo_out.start()
    for s in range(3):
        sent(s)
    for off in (1, 2, 3):
        pltpu.make_async_copy(near.at[0], near.at[0], scan_send.at[off - 1]).wait()

    for g in range(GROUPS - 1):

        @pl.when(g < grp)
        def _():
            pltpu.make_async_copy(far.at[g], far.at[g], far_sem.at[g]).wait()

        prefix = prefix + jnp.where(g < grp, far[g].astype(F32), 0.0)

    gain = gain_ref[pl.ds(core, 1), :]

    def normed(b):
        rows = pl.ds(pl.multiple_of(b * TOK, TOK), TOK)
        before = prefix + jnp.where(b == 1, state[0], 0.0)
        attended = intra[rows] + jnp.dot(
            q_act[rows].astype(BF16), before.astype(BF16), preferred_element_type=F32
        )
        meansq = jnp.mean(attended * attended, axis=-1, keepdims=True)
        return (attended * lax.rsqrt(meansq + 1e-06) * gain).astype(BF16)

    nrm_out[...] = normed(1 - core)
    nrm_copy = pltpu.make_async_remote_copy(
        src_ref=nrm_out, dst_ref=nrm.at[core], send_sem=pair_send.at[2], recv_sem=pair_recv.at[2],
        device_id=sibling, device_id_type=MESH,
    )
    nrm_copy.start()
    nrm[core] = normed(core)
    wo_out.wait()
    nrm_copy.wait()
    lhs = jnp.concatenate([nrm[0], nrm[1]], axis=1)
    stores = []
    for block in range(16):
        columns = pl.ds(block * BLK, BLK)
        out_buf[:, columns] = jnp.dot(lhs, wo[block], preferred_element_type=F32).astype(BF16)
        if block % 2 == 1:
            columns = pl.ds((block - 1) * BLK, 2 * BLK)
            copy = pltpu.make_async_copy(out_buf.at[:, columns], out_ref.at[:, columns], store_sem.at[block // 2])
            copy.start()
            stores.append(copy)
    for off in (1, 2, 3):

        @pl.when(grp + off < GROUPS)
        def _():
            pltpu.make_async_copy(total, total, scan_send.at[2 + off]).wait()

    for copy in stores:
        copy.wait()


def shards(tokens, w_qkv, norm_gain, w_out):
    hbm = pl.BlockSpec(memory_space=pl.ANY)
    dma = pltpu.SemaphoreType.DMA
    width = tokens.shape[2]
    out = pl.pallas_call(
        kernel,
        out_shape=jax.ShapeDtypeStruct((TOK, width), BF16),
        in_specs=[hbm, hbm, pl.BlockSpec(memory_space=pltpu.VMEM), hbm],
        out_specs=hbm,
        scratch_shapes=[
            pltpu.VMEM((2 * TOK, width), BF16),
            pltpu.VMEM((16, BLK, 2 * HEAD), BF16),
            pltpu.VMEM((16, BLK, HEAD), BF16),
            pltpu.VMEM((16, 2 * HEAD, BLK), BF16),
            pltpu.VMEM((2 * TOK, HEAD), BF16),
            pltpu.VMEM((2 * TOK, HEAD), BF16),
            pltpu.VMEM((2 * TOK, HEAD), F32),
            pltpu.VMEM((GROUP, HEAD, HEAD), BF16),
            pltpu.VMEM((GROUPS, HEAD, HEAD), BF16),
            pltpu.VMEM((HEAD, HEAD), BF16),
            pltpu.VMEM((2, TOK, HEAD), BF16),
            pltpu.VMEM((TOK, HEAD), BF16),
            pltpu.VMEM((TOK, width), BF16),
            pltpu.VMEM((2 * TOK, 2 * HEAD), F32),
            pltpu.VMEM((2 * TOK, HEAD), F32),
            pltpu.VMEM((2, HEAD, HEAD), F32),
            dma((5,)),
            dma((3,)),
            dma((3, 2, 16)),
            dma((3, 2, 16, 2)),
            dma((6,)),
            dma((GROUP,)),
            dma((GROUPS,)),
            dma((3,)),
            dma((3,)),
            dma((8,)),
        ],
        compiler_params=pltpu.CompilerParams(
            collective_id=0, has_side_effects=True, vmem_limit_bytes=48 * 1024 * 1024
        ),
        name="attention_layer",
    )(tokens[0], w_qkv, norm_gain.reshape(2, HEAD), w_out)
    return out[None]


def solution(mesh):
    return jax.shard_map(
        shards,
        mesh=mesh,
        in_specs=(P("dp", "seq", None), P("dp", None), P(), P(None, "dp")),
        out_specs=P("dp", "seq", None),
        check_vma=False,
    )
```

```python
import functools

import jax
import jax.numpy as jnp
from jax import lax
from jax.experimental import pallas as pl
from jax.experimental.pallas import tpu as pltpu
from jax.sharding import PartitionSpec as P

MESH = pl.DeviceIdType.MESH
BF16, F32 = jnp.bfloat16, jnp.float32
HEAD = 128
SIDE = 4
GROUP = 4
GROUPS = 4
TOK = 256
BLK = 256


def mod4(value):
    return lax.rem(value + 8, 4)


def kernel(
    tok_ref, w_ref, gain_ref, wo_ref, out_ref,
    x_buf, kv, q, wo, k_act, v_act, intra, near, far, total, nrm, nrm_out, out_buf, gain_buf,
    kv_acc, q_act, state,
    load_sem, send_sem, full_sem, half_sem, z_sem, scan_send, near_sem, far_sem, pair_send, pair_recv, wo_recv,
    store_sem, ready_sem,
):
    dp, seq = lax.axis_index("dp"), lax.axis_index("seq")
    y, x = lax.div(dp, SIDE), lax.rem(dp, SIDE)
    z, core = lax.div(seq, 2), lax.rem(seq, 2)
    grp, mem = lax.div(z, GROUP), lax.rem(z, GROUP)
    odd = lax.rem(z, 2)
    sibling = (dp, z * 2 + (1 - core))
    lane = pl.multiple_of(core * HEAD, HEAD)

    def at_xy(axis, off):
        if axis == 0:
            return (y * SIDE + mod4(x + off), seq)
        return (mod4(y + off) * SIDE + x, seq)

    def at_z(g, m):
        return (dp, (g * GROUP + m) * 2 + core)

    def along_z(off):
        return (dp, lax.rem(z + off + 16, 16) * 2 + core)

    own_tokens = x_buf.at[pl.ds(pl.multiple_of(core * TOK, TOK), TOK)]
    loads = [
        pltpu.make_async_copy(w_ref.at[:, pl.ds(2 * HEAD + lane, HEAD)], kv.at[dp, :, pl.ds(0, HEAD)], load_sem.at[0]),
        pltpu.make_async_copy(w_ref.at[:, pl.ds(4 * HEAD + lane, HEAD)], kv.at[dp, :, pl.ds(HEAD, HEAD)], load_sem.at[1]),
        pltpu.make_async_copy(w_ref.at[:, pl.ds(lane, HEAD)], q.at[dp], load_sem.at[2]),
        pltpu.make_async_copy(wo_ref.at[:, pl.ds(lane, HEAD)], wo.at[core, dp], load_sem.at[3]),
        pltpu.make_async_copy(tok_ref, own_tokens, load_sem.at[4]),
        pltpu.make_async_copy(gain_ref, gain_buf, load_sem.at[5]),
    ]
    for copy in loads:
        copy.start()
    far[...] = jnp.zeros_like(far)

    barrier = pltpu.get_barrier_semaphore()
    partners = [sibling]
    for off in (1, 2, 3):
        partners += [at_xy(0, off), at_xy(1, off)]
    for off in (1, 2, 3, 4):
        partners += [along_z(off), along_z(-off)]
    for partner in partners:
        pl.semaphore_signal(barrier, inc=1, device_id=partner, device_id_type=MESH)
    pl.semaphore_wait(barrier, len(partners))
    pl.semaphore_signal(ready_sem, inc=1, device_id=along_z(4), device_id_type=MESH)

    def piece(s, block, half, sub=None):
        if s == 0:
            rows = 96
            start = 160 * odd if half == 0 else 96 - 32 * odd
        else:
            rows = 128
            start = half * rows
        if sub is not None:
            start, rows = start + sub * (rows // 2), rows // 2
        start = pl.multiple_of(start, 16) if not isinstance(start, int) else start
        return (kv, q, wo.at[core])[s].at[block, pl.ds(start, rows)]

    def block_at(half, first, second):
        dy, dx = (second, first) if half == 0 else (first, second)
        return mod4(y + dy) * SIDE + mod4(x + dx)

    def send(ref, send_to, received, device):
        pltpu.make_async_remote_copy(
            src_ref=ref, dst_ref=ref, send_sem=send_to, recv_sem=received, device_id=device, device_id_type=MESH
        ).start()

    def wait(ref, sem):
        pltpu.make_async_copy(ref, ref, sem).wait()

    def send_full(s, half, block, axis, off):
        send(piece(s, block, half), send_sem.at[s], full_sem.at[s, half, block], at_xy(axis, off))

    def wait_full(s, half, block):
        wait(piece(s, block, half), full_sem.at[s, half, block])

    def send_half(s, half, block, sub, axis, off):
        send(piece(s, block, half, sub), send_sem.at[s], half_sem.at[s, half, block, sub], at_xy(axis, off))

    def wait_halves(s, half, block):
        for sub in (0, 1):
            wait(piece(s, block, half, sub), half_sem.at[s, half, block, sub])

    def z_rows(parity, block, part):
        return kv.at[block, pl.ds(pl.multiple_of(192 * parity + 32 * part, 32), 32)]

    def send_z(block):
        for part, off in ((0, 1), (1, -1)):
            send(z_rows(odd, block, part), send_sem.at[3], z_sem.at[block, part], along_z(off))

    def wait_z(block):
        for part in (0, 1):
            wait(z_rows(1 - odd, block, part), z_sem.at[block, part])

    def stage0(s):
        for half in (0, 1):
            for off in (1, -1):
                send_full(s, half, dp, half, off)
        if s == 0:
            for half in (0, 1):
                send_full(s, half, dp, half, 2)
        for half in (0, 1):
            for off in (1, -1):
                send_full(s, half, dp, 1 - half, off)

    def stage1(s):
        for first in (1, -1):
            for half in (0, 1):
                block = block_at(half, first, 0)
                wait_full(s, half, block)
                if s > 0:
                    send_half(s, half, block, 0 if first == -1 else 1, half, -first)
                for off in (1, -1):
                    send_full(s, half, block, 1 - half, off)
                if s == 0 and half == 0:
                    send_z(block)
        for half in (0, 1):
            block = block_at(half, 2, 0)
            if s == 0:
                wait_full(s, half, block)
            else:
                wait_halves(s, half, block)
            for off in (1, -1):
                send_full(s, half, block, 1 - half, off)
            if s == 0 and half == 0:
                send_z(block)

    def stage2(s):
        for first in (0, 1, -1, 2):
            for second in (-1, 1):
                for half in (0, 1):
                    block = block_at(half, first, second)
                    wait_full(s, half, block)
                    send_half(s, half, block, 0 if second == -1 else 1, 1 - half, -second)
                    if s == 0 and half == 0:
                        send_z(block)

    def sent(s):
        ref = (
            kv.at[pl.ds(0, 15), pl.ds(0, 192)],
            q.at[pl.ds(0, 15)],
            wo.at[0, pl.ds(0, 15)],
            kv.at[pl.ds(0, 15), pl.ds(0, 64)],
        )[s]
        wait(ref, send_sem.at[s])

    def project(weights, acc, part, first):
        wide = weights.shape[-1]
        term = jnp.dot(
            x_buf[:, pl.ds(pl.multiple_of(part * 1024, 1024), 1024)],
            weights[pl.ds(part * 4, 4)].reshape(1024, wide),
            preferred_element_type=F32,
        )
        if first:
            acc[...] = term
        else:
            acc[...] += term

    loads[0].wait()
    loads[1].wait()
    stage0(0)
    tokens_out = pltpu.make_async_remote_copy(
        src_ref=tok_ref, dst_ref=own_tokens,
        send_sem=pair_send.at[0], recv_sem=pair_recv.at[0], device_id=sibling, device_id_type=MESH,
    )
    tokens_out.start()
    stage1(0)
    stage2(0)
    loads[2].wait()
    stage0(1)
    for first in (0, 1, -1, 2):
        block = block_at(0, first, 2)
        wait_halves(0, 0, block)
        send_z(block)
    loads[3].wait()
    stage0(2)
    loads[4].wait()
    loads[5].wait()
    tokens_out.wait()

    for dy in (0, 1, -1, 2):
        wait_halves(0, 1, block_at(1, dy, 2))
        for dx in (0, 1, -1, 2):
            if (dy, dx) != (0, 0):
                wait_z(block_at(1, dy, dx))
        project(kv, kv_acc, mod4(y + dy), dy == 0)
    keys_in = kv_acc[:, :HEAD]
    k_act[...] = (keys_in / (1.0 + jnp.exp(-keys_in))).astype(BF16)
    v_act[...] = kv_acc[:, HEAD:].astype(BF16)
    for b in (0, 1):
        rows = pl.ds(b * TOK, TOK)
        state[b] = lax.dot_general(
            k_act[rows], v_act[rows], (((0,), (0,)), ((), ())), preferred_element_type=F32
        )
    near[mem] = (state[0] + state[1]).astype(BF16)

    for off in (1, 2, 3):
        send(near.at[mem], scan_send.at[off - 1], near_sem.at[mem], at_z(grp, mod4(mem + off)))
    stage1(1)
    stage1(2)
    for off in (1, 2, 3):
        m = mod4(mem + off)
        wait(near.at[m], near_sem.at[m])
    all_near = [near[m].astype(F32) for m in range(GROUP)]
    total[...] = (all_near[0] + all_near[1] + all_near[2] + all_near[3]).astype(BF16)

    pl.semaphore_wait(ready_sem, 1)
    for off in (2, 1, 3):
        g = grp + off

        @pl.when(g < GROUPS)
        def _():
            pltpu.make_async_remote_copy(
                src_ref=total, dst_ref=far.at[grp], send_sem=scan_send.at[2 + off], recv_sem=far_sem.at[grp],
                device_id=at_z(g, mem), device_id_type=MESH,
            ).start()

    prefix = jnp.zeros((HEAD, HEAD), F32)
    for m in range(GROUP - 1):
        prefix = prefix + jnp.where(m < mem, all_near[m], 0.0)

    def send_wo(block):
        send(wo.at[core, block], pair_send.at[1], wo_recv.at[block], sibling)

    inner = [(dy, dx) for dy in (0, 1, -1) for dx in (0, 1, -1)]
    outer = [(dy, 2) for dy in (0, 1, -1)] + [(2, dx) for dx in (0, 1, -1, 2)]
    stage2(1)
    stage2(2)
    for dy, dx in inner:
        send_wo(block_at(1, dy, dx))
    for half in (0, 1):
        for first in (0, 1, -1, 2):
            wait_halves(1, half, block_at(half, first, 2))
    for part in range(4):
        project(q, q_act, part, part == 0)
    queries = q_act[...]
    q_act[...] = queries / (1.0 + jnp.exp(-queries))
    causal = lax.broadcasted_iota(jnp.int32, (TOK, TOK), 0) >= lax.broadcasted_iota(jnp.int32, (TOK, TOK), 1)
    for b in (0, 1):
        rows = pl.ds(b * TOK, TOK)
        scores = lax.dot_general(
            q_act[rows].astype(BF16), k_act[rows], (((1,), (1,)), ((), ())), preferred_element_type=F32
        )
        scores = jnp.where(causal, scores, 0.0).astype(BF16)
        intra[rows] = jnp.dot(scores, v_act[rows], preferred_element_type=F32)
    for half in (0, 1):
        for first in (0, 1, -1, 2):
            wait_halves(2, half, block_at(half, first, 2))
    for dy, dx in outer:
        send_wo(block_at(1, dy, dx))
    for s in range(4):
        sent(s)
    for off in (1, 2, 3):
        wait(near.at[0], scan_send.at[off - 1])

    for g in range(GROUPS - 1):

        @pl.when(g < grp)
        def _():
            wait(far.at[g], far_sem.at[g])

        prefix = prefix + jnp.where(g < grp, far[g].astype(F32), 0.0)

    gain = gain_buf[pl.ds(core, 1), :]

    def normed(b):
        rows = pl.ds(pl.multiple_of(b * TOK, TOK), TOK)
        before = prefix + jnp.where(b == 1, state[0], 0.0)
        attended = intra[rows] + jnp.dot(
            q_act[rows].astype(BF16), before.astype(BF16), preferred_element_type=F32
        )
        meansq = jnp.mean(attended * attended, axis=-1, keepdims=True)
        return (attended * lax.rsqrt(meansq + 1e-06) * gain).astype(BF16)

    nrm_out[...] = normed(1 - core)
    nrm_copy = pltpu.make_async_remote_copy(
        src_ref=nrm_out, dst_ref=nrm.at[core], send_sem=pair_send.at[2], recv_sem=pair_recv.at[1],
        device_id=sibling, device_id_type=MESH,
    )
    nrm_copy.start()
    nrm[core] = normed(core)
    nrm_copy.wait()
    lhs = jnp.concatenate([nrm[0], nrm[1]], axis=1)
    stores = []
    for dy, dx in inner + outer:
        block = block_at(1, dy, dx)
        wait(wo.at[1 - core, block], wo_recv.at[block])
        columns = pl.ds(pl.multiple_of(block * BLK, BLK), BLK)
        weights = jnp.concatenate([wo[0, block], wo[1, block]], axis=1)
        out_buf[:, columns] = jnp.dot(lhs, weights, preferred_element_type=F32).astype(BF16)
        copy = pltpu.make_async_copy(out_buf.at[:, columns], out_ref.at[:, columns], store_sem.at[block])
        copy.start()
        stores.append(copy)
    wait(wo.at[core], pair_send.at[1])
    for off in (1, 2, 3):

        @pl.when(grp + off < GROUPS)
        def _():
            wait(total, scan_send.at[2 + off])

    for copy in stores:
        copy.wait()


def shards(tokens, w_qkv, norm_gain, w_out):
    hbm = pl.BlockSpec(memory_space=pl.ANY)
    dma = pltpu.SemaphoreType.DMA
    width = tokens.shape[2]
    out = pl.pallas_call(
        kernel,
        out_shape=jax.ShapeDtypeStruct((TOK, width), BF16),
        in_specs=[hbm] * 4,
        out_specs=hbm,
        scratch_shapes=[
            pltpu.VMEM((2 * TOK, width), BF16),
            pltpu.VMEM((16, BLK, 2 * HEAD), BF16),
            pltpu.VMEM((16, BLK, HEAD), BF16),
            pltpu.VMEM((2, 16, 2 * HEAD, BLK // 2), BF16),
            pltpu.VMEM((2 * TOK, HEAD), BF16),
            pltpu.VMEM((2 * TOK, HEAD), BF16),
            pltpu.VMEM((2 * TOK, HEAD), F32),
            pltpu.VMEM((GROUP, HEAD, HEAD), BF16),
            pltpu.VMEM((GROUPS, HEAD, HEAD), BF16),
            pltpu.VMEM((HEAD, HEAD), BF16),
            pltpu.VMEM((2, TOK, HEAD), BF16),
            pltpu.VMEM((TOK, HEAD), BF16),
            pltpu.VMEM((TOK, width), BF16),
            pltpu.VMEM((2, HEAD), F32),
            pltpu.VMEM((2 * TOK, 2 * HEAD), F32),
            pltpu.VMEM((2 * TOK, HEAD), F32),
            pltpu.VMEM((2, HEAD, HEAD), F32),
            dma((6,)),
            dma((4,)),
            dma((3, 2, 16)),
            dma((3, 2, 16, 2)),
            dma((16, 2)),
            dma((6,)),
            dma((GROUP,)),
            dma((GROUPS,)),
            dma((3,)),
            dma((2,)),
            dma((16,)),
            dma((16,)),
            pltpu.SemaphoreType.REGULAR,
        ],
        compiler_params=pltpu.CompilerParams(
            collective_id=0, has_side_effects=True, vmem_limit_bytes=48 * 1024 * 1024
        ),
        name="attention_layer",
    )(*(pltpu.with_memory_space_constraint(a, pltpu.HBM) for a in (tokens[0], w_qkv, norm_gain.reshape(2, HEAD), w_out)))
    return out[None]


def solution(mesh):
    return jax.shard_map(
        shards,
        mesh=mesh,
        in_specs=(P("dp", "seq", None), P("dp", None), P(), P(None, "dp")),
        out_specs=P("dp", "seq", None),
        check_vma=False,
    )
```

```python
import functools

import jax
import jax.numpy as jnp
from jax import lax
from jax.experimental import pallas as pl
from jax.experimental.pallas import tpu as pltpu
from jax.sharding import PartitionSpec as P

MESH = pl.DeviceIdType.MESH
BF16, F32 = jnp.bfloat16, jnp.float32
HEAD = 128
SIDE = 4
GROUP = 4
GROUPS = 4
TOK = 256
BLK = 256


def mod4(value):
    return lax.rem(value + 8, 4)


def kernel(
    tok_ref, w_ref, gain_ref, wo_ref, out_ref,
    x_buf, kv, qo, wo_pair, k_act, v_act, intra, near, far, total, nrm, nrm_out, out_buf, gain_buf,
    kv_acc, q_act, state,
    load_sem, send_sem, full_sem, half_sem, z_sem, scan_send, near_sem, far_sem, pair_send, pair_recv, wo_recv,
    store_sem, ready_sem,
):
    dp, seq = lax.axis_index("dp"), lax.axis_index("seq")
    y, x = lax.div(dp, SIDE), lax.rem(dp, SIDE)
    z, core = lax.div(seq, 2), lax.rem(seq, 2)
    grp, mem = lax.div(z, GROUP), lax.rem(z, GROUP)
    odd = lax.rem(z, 2)
    sibling = (dp, z * 2 + (1 - core))
    lane = pl.multiple_of(core * HEAD, HEAD)

    def at_xy(axis, off):
        if axis == 0:
            return (y * SIDE + mod4(x + off), seq)
        return (mod4(y + off) * SIDE + x, seq)

    def at_z(g, m):
        return (dp, (g * GROUP + m) * 2 + core)

    def along_z(off):
        return (dp, lax.rem(z + off + 16, 16) * 2 + core)

    own_tokens = x_buf.at[pl.ds(pl.multiple_of(core * TOK, TOK), TOK)]
    loads = [
        pltpu.make_async_copy(w_ref.at[:, pl.ds(2 * HEAD + lane, HEAD)], kv.at[dp, :, pl.ds(0, HEAD)], load_sem.at[0]),
        pltpu.make_async_copy(w_ref.at[:, pl.ds(4 * HEAD + lane, HEAD)], kv.at[dp, :, pl.ds(HEAD, HEAD)], load_sem.at[1]),
        pltpu.make_async_copy(w_ref.at[:, pl.ds(lane, HEAD)], qo.at[dp, 0], load_sem.at[2]),
        pltpu.make_async_copy(wo_ref.at[:, pl.ds(lane, HEAD)], qo.at[dp, 1], load_sem.at[3]),
        pltpu.make_async_copy(tok_ref, own_tokens, load_sem.at[4]),
        pltpu.make_async_copy(gain_ref, gain_buf, load_sem.at[5]),
    ]
    for copy in loads:
        copy.start()
    far[...] = jnp.zeros_like(far)

    barrier = pltpu.get_barrier_semaphore()
    partners = [sibling]
    for off in (1, 2, 3):
        partners += [at_xy(0, off), at_xy(1, off)]
    partners += [along_z(1), along_z(-1)]
    for partner in partners:
        pl.semaphore_signal(barrier, inc=1, device_id=partner, device_id_type=MESH)
    pl.semaphore_wait(barrier, len(partners))

    def tell(n):
        for off in (2**n, -(2**n)):
            pl.semaphore_signal(ready_sem.at[n], inc=1, device_id=along_z(off), device_id_type=MESH)

    def hear(n):
        pl.semaphore_wait(ready_sem.at[n], 2)

    def piece(s, block, half, sub=None):
        if s == 0:
            rows = 96
            start = 160 * odd if half == 0 else 96 - 32 * odd
        else:
            rows = 128
            start = half * rows
        if sub is not None:
            start, rows = start + sub * (rows // 2), rows // 2
        start = pl.multiple_of(start, 16) if not isinstance(start, int) else start
        return kv.at[block, pl.ds(start, rows)] if s == 0 else qo.at[block, :, pl.ds(start, rows)]

    def block_at(half, first, second):
        dy, dx = (second, first) if half == 0 else (first, second)
        return mod4(y + dy) * SIDE + mod4(x + dx)

    def send(ref, send_to, received, device):
        pltpu.make_async_remote_copy(
            src_ref=ref, dst_ref=ref, send_sem=send_to, recv_sem=received, device_id=device, device_id_type=MESH
        ).start()

    def wait(ref, sem):
        pltpu.make_async_copy(ref, ref, sem).wait()

    def send_full(s, half, block, axis, off):
        send(piece(s, block, half), send_sem.at[s], full_sem.at[s, half, block], at_xy(axis, off))

    def wait_full(s, half, block):
        wait(piece(s, block, half), full_sem.at[s, half, block])

    def send_half(s, half, block, sub, axis, off):
        send(piece(s, block, half, sub), send_sem.at[s], half_sem.at[s, half, block, sub], at_xy(axis, off))

    def wait_halves(s, half, block):
        for sub in (0, 1):
            wait(piece(s, block, half, sub), half_sem.at[s, half, block, sub])

    def z_rows(parity, block, part):
        return kv.at[block, pl.ds(pl.multiple_of(192 * parity + 32 * part, 32), 32)]

    def send_z(block):
        for part, off in ((0, 1), (1, -1)):
            send(z_rows(odd, block, part), send_sem.at[3], z_sem.at[block, part], along_z(off))

    def wait_z(block):
        for part in (0, 1):
            wait(z_rows(1 - odd, block, part), z_sem.at[block, part])

    def stage0(s):
        for half in (0, 1):
            for off in (1, -1):
                send_full(s, half, dp, half, off)
        for half in (0, 1):
            send_full(s, half, dp, half, 2)
        for half in (0, 1):
            for off in (1, -1):
                send_full(s, half, dp, 1 - half, off)

    def stage1(s):
        for first in (1, -1, 2):
            for half in (0, 1):
                block = block_at(half, first, 0)
                wait_full(s, half, block)
                for off in (1, -1):
                    send_full(s, half, block, 1 - half, off)
                if s == 0 and half == 0:
                    send_z(block)

    def stage2(s):
        for first in (0, 1, -1, 2):
            for second in (-1, 1):
                for half in (0, 1):
                    block = block_at(half, first, second)
                    wait_full(s, half, block)
                    send_half(s, half, block, 0 if second == -1 else 1, 1 - half, -second)
                    if s == 0 and half == 0:
                        send_z(block)

    def sent(s):
        ref = (kv.at[pl.ds(0, 15), pl.ds(0, 192)], qo.at[pl.ds(0, 15)], None, kv.at[pl.ds(0, 15), pl.ds(0, 64)])[s]
        wait(ref, send_sem.at[s])

    def project(weights, acc, part, first):
        term = jnp.dot(
            x_buf[:, pl.ds(pl.multiple_of(part * 1024, 1024), 1024)], weights.reshape(1024, -1), preferred_element_type=F32
        )
        if first:
            acc[...] = term
        else:
            acc[...] += term

    loads[0].wait()
    loads[1].wait()
    stage0(0)
    tokens_out = pltpu.make_async_remote_copy(
        src_ref=tok_ref, dst_ref=own_tokens,
        send_sem=pair_send.at[0], recv_sem=pair_recv.at[0], device_id=sibling, device_id_type=MESH,
    )
    tokens_out.start()
    tell(0)
    stage1(0)
    hear(0)
    tell(1)
    stage2(0)
    loads[2].wait()
    loads[3].wait()
    stage0(1)
    hear(1)
    tell(2)
    for first in (0, 1, -1, 2):
        block = block_at(0, first, 2)
        wait_halves(0, 0, block)
        send_z(block)
    stage1(1)
    hear(2)
    loads[4].wait()
    loads[5].wait()
    tokens_out.wait()

    for dy in (0, 1, -1, 2):
        wait_halves(0, 1, block_at(1, dy, 2))
        for dx in (0, 1, -1, 2):
            if (dy, dx) != (0, 0):
                wait_z(block_at(1, dy, dx))
        part = mod4(y + dy)
        project(kv[pl.ds(part * 4, 4)], kv_acc, part, dy == 0)
    keys_in = kv_acc[:, :HEAD]
    k_act[...] = (keys_in / (1.0 + jnp.exp(-keys_in))).astype(BF16)
    v_act[...] = kv_acc[:, HEAD:].astype(BF16)
    for b in (0, 1):
        rows = pl.ds(b * TOK, TOK)
        state[b] = lax.dot_general(
            k_act[rows], v_act[rows], (((0,), (0,)), ((), ())), preferred_element_type=F32
        )
    near[mem] = (state[0] + state[1]).astype(BF16)

    for off in (1, 2, 3):
        send(near.at[mem], scan_send.at[off - 1], near_sem.at[mem], at_z(grp, mod4(mem + off)))
    for off in (1, 2, 3):
        m = mod4(mem + off)
        wait(near.at[m], near_sem.at[m])
    all_near = [near[m].astype(F32) for m in range(GROUP)]
    total[...] = (all_near[0] + all_near[1] + all_near[2] + all_near[3]).astype(BF16)

    targets = [(2, 3, 0), (2, 0, 3), (2, 3, 1), (2, 0, 2), (1, None, None), (3, None, None)]

    def sends_total(off, member):
        inside = grp + off < GROUPS
        return inside if member is None else jnp.logical_and(inside, mem == member)

    for n, (off, member, target) in enumerate(targets):

        @pl.when(sends_total(off, member))
        def _():
            pltpu.make_async_remote_copy(
                src_ref=total, dst_ref=far.at[grp], send_sem=scan_send.at[3 + n], recv_sem=far_sem.at[grp],
                device_id=at_z(grp + off, mem if target is None else target), device_id_type=MESH,
            ).start()

    prefix = jnp.zeros((HEAD, HEAD), F32)
    for m in range(GROUP - 1):
        prefix = prefix + jnp.where(m < mem, all_near[m], 0.0)

    def send_wo(block):
        pltpu.make_async_remote_copy(
            src_ref=qo.at[block, 1], dst_ref=wo_pair.at[block], send_sem=pair_send.at[1], recv_sem=wo_recv.at[block],
            device_id=sibling, device_id_type=MESH,
        ).start()

    inner = [(dy, dx) for dy in (0, 1, -1) for dx in (0, 1, -1)]
    outer = [(dy, 2) for dy in (0, 1, -1)] + [(2, dx) for dx in (0, 1, -1, 2)]
    stage2(1)
    for dy, dx in inner:
        send_wo(block_at(1, dy, dx))
    for half in (0, 1):
        for first in (0, 1, -1, 2):
            wait_halves(1, half, block_at(half, first, 2))
    for dy, dx in outer:
        send_wo(block_at(1, dy, dx))
    for part in range(4):
        project(qo[pl.ds(part * 4, 4), 0], q_act, part, part == 0)
    queries = q_act[...]
    q_act[...] = queries / (1.0 + jnp.exp(-queries))
    causal = lax.broadcasted_iota(jnp.int32, (TOK, TOK), 0) >= lax.broadcasted_iota(jnp.int32, (TOK, TOK), 1)
    for b in (0, 1):
        rows = pl.ds(b * TOK, TOK)
        scores = lax.dot_general(
            q_act[rows].astype(BF16), k_act[rows], (((1,), (1,)), ((), ())), preferred_element_type=F32
        )
        scores = jnp.where(causal, scores, 0.0).astype(BF16)
        intra[rows] = jnp.dot(scores, v_act[rows], preferred_element_type=F32)
    for s in (0, 1, 3):
        sent(s)
    for off in (1, 2, 3):
        wait(near.at[0], scan_send.at[off - 1])

    for g in range(GROUPS - 1):

        @pl.when(g < grp)
        def _():
            wait(far.at[g], far_sem.at[g])

        prefix = prefix + jnp.where(g < grp, far[g].astype(F32), 0.0)

    gain = gain_buf[pl.ds(core, 1), :]

    def normed(b):
        rows = pl.ds(pl.multiple_of(b * TOK, TOK), TOK)
        before = prefix + jnp.where(b == 1, state[0], 0.0)
        attended = intra[rows] + jnp.dot(
            q_act[rows].astype(BF16), before.astype(BF16), preferred_element_type=F32
        )
        meansq = jnp.mean(attended * attended, axis=-1, keepdims=True)
        return (attended * lax.rsqrt(meansq + 1e-06) * gain).astype(BF16)

    nrm_out[...] = normed(1 - core)
    nrm_copy = pltpu.make_async_remote_copy(
        src_ref=nrm_out, dst_ref=nrm.at[core], send_sem=pair_send.at[2], recv_sem=pair_recv.at[1],
        device_id=sibling, device_id_type=MESH,
    )
    nrm_copy.start()
    nrm[core] = normed(core)
    nrm_copy.wait()
    lhs = jnp.concatenate([nrm[0], nrm[1]], axis=1)
    stores = []
    for dy, dx in inner + outer:
        block = block_at(1, dy, dx)
        wait(wo_pair.at[block], wo_recv.at[block])
        columns = pl.ds(pl.multiple_of(block * BLK, BLK), BLK)
        own, other = qo[block, 1], wo_pair[block]
        weights = jnp.concatenate([jnp.where(core == 0, own, other), jnp.where(core == 0, other, own)], axis=1)
        out_buf[:, columns] = jnp.dot(lhs, weights, preferred_element_type=F32).astype(BF16)
        copy = pltpu.make_async_copy(out_buf.at[:, columns], out_ref.at[:, columns], store_sem.at[block])
        copy.start()
        stores.append(copy)
    wait(wo_pair, pair_send.at[1])
    for n, (off, member, _) in enumerate(targets):

        @pl.when(sends_total(off, member))
        def _():
            wait(total, scan_send.at[3 + n])

    for copy in stores:
        copy.wait()


def shards(tokens, w_qkv, norm_gain, w_out):
    hbm = pl.BlockSpec(memory_space=pl.ANY)
    dma = pltpu.SemaphoreType.DMA
    width = tokens.shape[2]
    out = pl.pallas_call(
        kernel,
        out_shape=jax.ShapeDtypeStruct((TOK, width), BF16),
        in_specs=[hbm] * 4,
        out_specs=hbm,
        scratch_shapes=[
            pltpu.VMEM((2 * TOK, width), BF16),
            pltpu.VMEM((16, BLK, 2 * HEAD), BF16),
            pltpu.VMEM((16, 2, BLK, HEAD), BF16),
            pltpu.VMEM((16, BLK, HEAD), BF16),
            pltpu.VMEM((2 * TOK, HEAD), BF16),
            pltpu.VMEM((2 * TOK, HEAD), BF16),
            pltpu.VMEM((2 * TOK, HEAD), F32),
            pltpu.VMEM((GROUP, HEAD, HEAD), BF16),
            pltpu.VMEM((GROUPS, HEAD, HEAD), BF16),
            pltpu.VMEM((HEAD, HEAD), BF16),
            pltpu.VMEM((2, TOK, HEAD), BF16),
            pltpu.VMEM((TOK, HEAD), BF16),
            pltpu.VMEM((TOK, width), BF16),
            pltpu.VMEM((2, HEAD), F32),
            pltpu.VMEM((2 * TOK, 2 * HEAD), F32),
            pltpu.VMEM((2 * TOK, HEAD), F32),
            pltpu.VMEM((2, HEAD, HEAD), F32),
            dma((6,)),
            dma((4,)),
            dma((2, 2, 16)),
            dma((2, 2, 16, 2)),
            dma((16, 2)),
            dma((9,)),
            dma((GROUP,)),
            dma((GROUPS,)),
            dma((3,)),
            dma((2,)),
            dma((16,)),
            dma((16,)),
            pltpu.SemaphoreType.REGULAR((3,)),
        ],
        compiler_params=pltpu.CompilerParams(
            collective_id=0, has_side_effects=True, vmem_limit_bytes=48 * 1024 * 1024
        ),
        name="attention_layer",
    )(*(pltpu.with_memory_space_constraint(a, pltpu.HBM) for a in (tokens[0], w_qkv, norm_gain.reshape(2, HEAD), w_out)))
    return out[None]


def solution(mesh):
    return jax.shard_map(
        shards,
        mesh=mesh,
        in_specs=(P("dp", "seq", None), P("dp", None), P(), P(None, "dp")),
        out_specs=P("dp", "seq", None),
        check_vma=False,
    )
```

```python
import functools

import jax
import jax.numpy as jnp
from jax import lax
from jax.experimental import pallas as pl
from jax.experimental.pallas import tpu as pltpu
from jax.sharding import PartitionSpec as P

MESH = pl.DeviceIdType.MESH
BF16, F32 = jnp.bfloat16, jnp.float32
HEAD = 128
SIDE = 4
GROUP = 4
GROUPS = 4
TOK = 256
BLK = 256


OFFSETS = (0, 1, -1, 2)


def slot_of(off):
    return OFFSETS.index(2 if off in (2, -2) else off)


def mod4(value):
    return lax.rem(value + 8, 4)


def kernel(
    tok_ref, w_ref, gain_ref, wo_ref, out_ref,
    x_buf, kv, qo, wo_pair, k_act, v_act, intra, near, far, total, nrm, nrm_out, out_buf, gain_buf,
    kv_acc, q_act, state,
    load_sem, send_sem, first_sem, second_sem, third_sem, scan_send, near_sem, far_sem, pair_send, pair_recv, wo_recv,
    store_sem, ready_sem,
):
    dp, seq = lax.axis_index("dp"), lax.axis_index("seq")
    y, x = lax.div(dp, SIDE), lax.rem(dp, SIDE)
    z, core = lax.div(seq, 2), lax.rem(seq, 2)
    grp, mem = lax.div(z, GROUP), lax.rem(z, GROUP)
    sibling = (dp, z * 2 + (1 - core))
    lane = pl.multiple_of(core * HEAD, HEAD)

    def at_xy(axis, off):
        if axis == 0:
            return (y * SIDE + mod4(x + off), seq)
        return (mod4(y + off) * SIDE + x, seq)

    def at_z(g, m):
        return (dp, (g * GROUP + m) * 2 + core)

    def along_z(off):
        return (dp, lax.rem(z + off + 16, 16) * 2 + core)

    own_tokens = x_buf.at[pl.ds(pl.multiple_of(core * TOK, TOK), TOK)]
    loads = [
        pltpu.make_async_copy(w_ref.at[:, pl.ds(2 * HEAD + lane, HEAD)], kv.at[0, 0, :, pl.ds(0, HEAD)], load_sem.at[0]),
        pltpu.make_async_copy(w_ref.at[:, pl.ds(4 * HEAD + lane, HEAD)], kv.at[0, 0, :, pl.ds(HEAD, HEAD)], load_sem.at[1]),
        pltpu.make_async_copy(w_ref.at[:, pl.ds(lane, HEAD)], qo.at[0, 0, 0], load_sem.at[2]),
        pltpu.make_async_copy(wo_ref.at[:, pl.ds(lane, HEAD)], qo.at[0, 0, 1], load_sem.at[3]),
        pltpu.make_async_copy(tok_ref, own_tokens, load_sem.at[4]),
        pltpu.make_async_copy(gain_ref, gain_buf, load_sem.at[5]),
    ]
    for copy in loads:
        copy.start()
    far[...] = jnp.zeros_like(far)

    barrier = pltpu.get_barrier_semaphore()
    partners = [sibling]
    for off in (1, 2, 3):
        partners += [at_xy(0, off), at_xy(1, off)]
    partners += [along_z(1), along_z(-1)]
    for partner in partners:
        pl.semaphore_signal(barrier, inc=1, device_id=partner, device_id_type=MESH)
    pl.semaphore_wait(barrier, len(partners))

    def tell(n):
        for off in (2**n, -(2**n)):
            pl.semaphore_signal(ready_sem.at[n], inc=1, device_id=along_z(off), device_id_type=MESH)

    def hear(n):
        pl.semaphore_wait(ready_sem.at[n], 2)

    def part_of(s, half, first, second, sub=None):
        rows = BLK // 2
        start = half * rows
        if sub is not None:
            start, rows = start + sub * (rows // 2), rows // 2
        at = (second, first) if half == 0 else (first, second)
        if s == 0:
            return kv.at[(*at, pl.ds(start, rows))]
        return qo.at[(*at, slice(None), pl.ds(start, rows))]

    rest = pl.ds(1, 3)

    def send(src, dst, send_to, received, device):
        pltpu.make_async_remote_copy(
            src_ref=src, dst_ref=dst, send_sem=send_to, recv_sem=received, device_id=device, device_id_type=MESH
        ).start()

    def wait(ref, sem):
        pltpu.make_async_copy(ref, ref, sem).wait()

    def start_first(s):
        for off in (1, -1, 2):
            for half in (0, 1):
                to = slot_of(-off)
                send(part_of(s, half, 0, 0), part_of(s, half, to, 0), send_sem.at[s], first_sem.at[s, half, to], at_xy(half, off))

    def start_second(s):
        for half in (0, 1):
            for off in (1, -1):
                to = slot_of(-off)
                send(part_of(s, half, 0, 0), part_of(s, half, 0, to), send_sem.at[s], second_sem.at[s, half, 0, to], at_xy(1 - half, off))

    def wait_first(s, half, first):
        wait(part_of(s, half, first, 0), first_sem.at[s, half, first])

    def pass_second(s, half, first, index):
        for off in (1, -1):
            to = slot_of(-off)
            send(
                part_of(s, half, first, 0), part_of(s, half, first, to), send_sem.at[s],
                second_sem.at[s, half, index, to], at_xy(1 - half, off),
            )

    def wait_second(s, half, first, index, second):
        wait(part_of(s, half, first, second), second_sem.at[s, half, index, second])

    def pass_third(s, half, first, index, second):
        sub = 0 if OFFSETS[second] == -1 else 1
        send(
            part_of(s, half, first, second, sub), part_of(s, half, first, 3, sub), send_sem.at[s],
            third_sem.at[s, half, index, sub], at_xy(1 - half, -OFFSETS[second]),
        )

    def wait_third(s, half, first, index):
        for sub in (0, 1):
            wait(part_of(s, half, first, 3, sub), third_sem.at[s, half, index, sub])

    def sent(s):
        rows = pl.ds(0, BLK * 15 // 16)
        wait(kv.at[:, :, rows] if s == 0 else qo.at[:, :, :, rows], send_sem.at[s])

    def block_at(a, b):
        return mod4(y + OFFSETS[a]) * SIDE + mod4(x + OFFSETS[b])

    def project(weights, acc, a):
        tokens = [x_buf[:, pl.ds(pl.multiple_of(block_at(a, b) * BLK, BLK), BLK)] for b in range(4)]
        term = jnp.dot(
            jnp.concatenate(tokens, axis=1), weights.reshape(SIDE * BLK, weights.shape[-1]), preferred_element_type=F32
        )
        if a == 0:
            acc[...] = term
        else:
            acc[...] += term

    loads[0].wait()
    loads[1].wait()
    start_first(0)
    start_second(0)
    tokens_out = pltpu.make_async_remote_copy(
        src_ref=tok_ref, dst_ref=own_tokens,
        send_sem=pair_send.at[0], recv_sem=pair_recv.at[0], device_id=sibling, device_id_type=MESH,
    )
    tokens_out.start()
    tell(0)
    for first in (1, 2, 3):
        for half in (0, 1):
            wait_first(0, half, first)
            pass_second(0, half, first, first)
    hear(0)
    tell(1)
    loads[2].wait()
    loads[3].wait()
    start_first(1)
    for half in (0, 1):
        for second in (1, 2):
            wait_second(0, half, 0, 0, second)
            pass_third(0, half, 0, 0, second)
    start_second(1)
    for half in (0, 1):
        for second in (1, 2):
            for first in (1, 2, 3):
                wait_second(0, half, first, first, second)
            pass_third(0, half, rest, 1, second)
    hear(1)
    tell(2)
    for half in (0, 1):
        for first in (1, 2, 3):
            wait_first(1, half, first)
        pass_second(1, half, rest, 1)
    hear(2)
    loads[4].wait()
    loads[5].wait()
    tokens_out.wait()

    for a in range(4):
        if a < 2:
            wait_third(0, 1, rest if a else 0, a)
        elif a == 3:
            wait_third(0, 0, 0, 0)
            wait_third(0, 0, rest, 1)
        project(kv[a], kv_acc, a)
    keys_in = kv_acc[:, :HEAD]
    k_act[...] = (keys_in / (1.0 + jnp.exp(-keys_in))).astype(BF16)
    v_act[...] = kv_acc[:, HEAD:].astype(BF16)
    for b in (0, 1):
        rows = pl.ds(b * TOK, TOK)
        state[b] = lax.dot_general(
            k_act[rows], v_act[rows], (((0,), (0,)), ((), ())), preferred_element_type=F32
        )
    near[mem] = (state[0] + state[1]).astype(BF16)

    for off in (1, 2, 3):
        send(near.at[mem], near.at[mem], scan_send.at[off - 1], near_sem.at[mem], at_z(grp, mod4(mem + off)))
    for half in (0, 1):
        for second in (1, 2):
            wait_second(1, half, 0, 0, second)
            wait_second(1, half, rest, 1, second)
            pass_third(1, half, pl.ds(0, 4), 0, second)

    def send_wo(n, rows, columns):
        send(qo.at[rows, columns, 1], wo_pair.at[rows, columns], pair_send.at[1 + n], wo_recv.at[n], sibling)

    inner = pl.ds(0, 3)
    shares = [(inner, inner), (inner, 3), (3, pl.ds(0, 4))]
    send_wo(0, *shares[0])
    for off in (1, 2, 3):
        m = mod4(mem + off)
        wait(near.at[m], near_sem.at[m])
    all_near = [near[m].astype(F32) for m in range(GROUP)]
    total[...] = (all_near[0] + all_near[1] + all_near[2] + all_near[3]).astype(BF16)

    targets = [(2, 3, 0), (2, 0, 3), (2, 3, 1), (2, 0, 2), (1, None, None), (3, None, None)]

    def sends_total(off, member):
        inside = grp + off < GROUPS
        return inside if member is None else jnp.logical_and(inside, mem == member)

    for n, (off, member, target) in enumerate(targets):

        @pl.when(sends_total(off, member))
        def _():
            pltpu.make_async_remote_copy(
                src_ref=total, dst_ref=far.at[grp], send_sem=scan_send.at[3 + n], recv_sem=far_sem.at[grp],
                device_id=at_z(grp + off, mem if target is None else target), device_id_type=MESH,
            ).start()

    prefix = jnp.zeros((HEAD, HEAD), F32)
    for m in range(GROUP - 1):
        prefix = prefix + jnp.where(m < mem, all_near[m], 0.0)

    for half in (0, 1):
        wait_third(1, half, pl.ds(0, 4), 0)
    for n in (1, 2):
        send_wo(n, *shares[n])
    for a in range(4):
        project(qo[a, :, 0], q_act, a)
    queries = q_act[...]
    q_act[...] = queries / (1.0 + jnp.exp(-queries))
    causal = lax.broadcasted_iota(jnp.int32, (TOK, TOK), 0) >= lax.broadcasted_iota(jnp.int32, (TOK, TOK), 1)
    for b in (0, 1):
        rows = pl.ds(b * TOK, TOK)
        scores = lax.dot_general(
            q_act[rows].astype(BF16), k_act[rows], (((1,), (1,)), ((), ())), preferred_element_type=F32
        )
        scores = jnp.where(causal, scores, 0.0).astype(BF16)
        intra[rows] = jnp.dot(scores, v_act[rows], preferred_element_type=F32)
    for s in (0, 1):
        sent(s)
    for off in (1, 2, 3):
        wait(near.at[0], scan_send.at[off - 1])

    for g in range(GROUPS - 1):

        @pl.when(g < grp)
        def _():
            wait(far.at[g], far_sem.at[g])

        prefix = prefix + jnp.where(g < grp, far[g].astype(F32), 0.0)

    gain = gain_buf[pl.ds(core, 1), :]

    def normed(b):
        rows = pl.ds(pl.multiple_of(b * TOK, TOK), TOK)
        before = prefix + jnp.where(b == 1, state[0], 0.0)
        attended = intra[rows] + jnp.dot(
            q_act[rows].astype(BF16), before.astype(BF16), preferred_element_type=F32
        )
        meansq = jnp.mean(attended * attended, axis=-1, keepdims=True)
        return (attended * lax.rsqrt(meansq + 1e-06) * gain).astype(BF16)

    nrm_out[...] = normed(1 - core)
    nrm_copy = pltpu.make_async_remote_copy(
        src_ref=nrm_out, dst_ref=nrm.at[core], send_sem=pair_send.at[4], recv_sem=pair_recv.at[1],
        device_id=sibling, device_id_type=MESH,
    )
    nrm_copy.start()
    nrm[core] = normed(core)
    nrm_copy.wait()
    lhs = jnp.concatenate([nrm[0], nrm[1]], axis=1)
    stores = []
    order = [(a, b) for a in range(3) for b in range(3)] + [(a, 3) for a in range(3)] + [(3, b) for b in range(4)]
    for n, (a, b) in enumerate(order):
        if n in (0, 9, 12):
            share = (0, 9, 12).index(n)
            wait(wo_pair.at[shares[share]], wo_recv.at[share])
        block = block_at(a, b)
        columns = pl.ds(pl.multiple_of(block * BLK, BLK), BLK)
        own, other = qo[a, b, 1], wo_pair[a, b]
        weights = jnp.concatenate([jnp.where(core == 0, own, other), jnp.where(core == 0, other, own)], axis=1)
        out_buf[:, columns] = jnp.dot(lhs, weights, preferred_element_type=F32).astype(BF16)
        copy = pltpu.make_async_copy(out_buf.at[:, columns], out_ref.at[:, columns], store_sem.at[n])
        copy.start()
        stores.append(copy)
    for n, share in enumerate(shares):
        wait(wo_pair.at[share], pair_send.at[1 + n])
    for n, (off, member, _) in enumerate(targets):

        @pl.when(sends_total(off, member))
        def _():
            wait(total, scan_send.at[3 + n])

    for copy in stores:
        copy.wait()


def shards(tokens, w_qkv, norm_gain, w_out):
    hbm = pl.BlockSpec(memory_space=pl.ANY)
    dma = pltpu.SemaphoreType.DMA
    width = tokens.shape[2]
    out = pl.pallas_call(
        kernel,
        out_shape=jax.ShapeDtypeStruct((TOK, width), BF16),
        in_specs=[hbm] * 4,
        out_specs=hbm,
        scratch_shapes=[
            pltpu.VMEM((2 * TOK, width), BF16),
            pltpu.VMEM((SIDE, SIDE, BLK, 2 * HEAD), BF16),
            pltpu.VMEM((SIDE, SIDE, 2, BLK, HEAD), BF16),
            pltpu.VMEM((SIDE, SIDE, BLK, HEAD), BF16),
            pltpu.VMEM((2 * TOK, HEAD), BF16),
            pltpu.VMEM((2 * TOK, HEAD), BF16),
            pltpu.VMEM((2 * TOK, HEAD), F32),
            pltpu.VMEM((GROUP, HEAD, HEAD), BF16),
            pltpu.VMEM((GROUPS, HEAD, HEAD), BF16),
            pltpu.VMEM((HEAD, HEAD), BF16),
            pltpu.VMEM((2, TOK, HEAD), BF16),
            pltpu.VMEM((TOK, HEAD), BF16),
            pltpu.VMEM((TOK, width), BF16),
            pltpu.VMEM((2, HEAD), F32),
            pltpu.VMEM((2 * TOK, 2 * HEAD), F32),
            pltpu.VMEM((2 * TOK, HEAD), F32),
            pltpu.VMEM((2, HEAD, HEAD), F32),
            dma((6,)),
            dma((2,)),
            dma((2, 2, 4)),
            dma((2, 2, 4, 3)),
            dma((2, 2, 2, 2)),
            dma((9,)),
            dma((GROUP,)),
            dma((GROUPS,)),
            dma((5,)),
            dma((2,)),
            dma((3,)),
            dma((16,)),
            pltpu.SemaphoreType.REGULAR((3,)),
        ],
        compiler_params=pltpu.CompilerParams(
            collective_id=0, has_side_effects=True, vmem_limit_bytes=48 * 1024 * 1024
        ),
        name="attention_layer",
    )(*(pltpu.with_memory_space_constraint(a, pltpu.HBM) for a in (tokens[0], w_qkv, norm_gain.reshape(2, HEAD), w_out)))
    return out[None]


def solution(mesh):
    return jax.shard_map(
        shards,
        mesh=mesh,
        in_specs=(P("dp", "seq", None), P("dp", None), P(), P(None, "dp")),
        out_specs=P("dp", "seq", None),
        check_vma=False,
    )
```

```python
import functools

import jax
import jax.numpy as jnp
from jax import lax
from jax.experimental import pallas as pl
from jax.experimental.pallas import tpu as pltpu
from jax.sharding import PartitionSpec as P

MESH = pl.DeviceIdType.MESH
BF16, F32 = jnp.bfloat16, jnp.float32
HEAD = 128
SIDE = 4
GROUP = 4
GROUPS = 4
TOK = 256
BLK = 256


OFFSETS = (0, 1, -1, 2)


def slot_of(off):
    return OFFSETS.index(2 if off in (2, -2) else off)


def mod4(value):
    return lax.rem(value + 8, 4)


def kernel(
    tok_ref, w_ref, gain_ref, wo_ref, out_ref,
    x_buf, kv, qo, wo_pair, k_act, v_act, intra, near, far, total, nrm, nrm_out, out_buf, gain_buf,
    kv_acc, q_act, state,
    load_sem, send_sem, first_sem, second_sem, third_sem, scan_send, near_sem, far_sem, pair_send, pair_recv, wo_recv,
    store_sem, ready_sem,
):
    dp, seq = lax.axis_index("dp"), lax.axis_index("seq")
    y, x = lax.div(dp, SIDE), lax.rem(dp, SIDE)
    z, core = lax.div(seq, 2), lax.rem(seq, 2)
    grp, mem = lax.div(z, GROUP), lax.rem(z, GROUP)
    sibling = (dp, z * 2 + (1 - core))
    lane = pl.multiple_of(core * HEAD, HEAD)

    def at_xy(axis, off):
        if axis == 0:
            return (y * SIDE + mod4(x + off), seq)
        return (mod4(y + off) * SIDE + x, seq)

    def at_z(g, m):
        return (dp, (g * GROUP + m) * 2 + core)

    def along_z(off):
        return (dp, lax.rem(z + off + 16, 16) * 2 + core)

    own_tokens = x_buf.at[pl.ds(pl.multiple_of(core * TOK, TOK), TOK)]
    loads = [
        pltpu.make_async_copy(w_ref.at[:, pl.ds(2 * HEAD + lane, HEAD)], kv.at[0, 0, :, pl.ds(0, HEAD)], load_sem.at[0]),
        pltpu.make_async_copy(w_ref.at[:, pl.ds(4 * HEAD + lane, HEAD)], kv.at[0, 0, :, pl.ds(HEAD, HEAD)], load_sem.at[1]),
        pltpu.make_async_copy(w_ref.at[:, pl.ds(lane, HEAD)], qo.at[0, 0, 0], load_sem.at[2]),
        pltpu.make_async_copy(wo_ref.at[:, pl.ds(lane, HEAD)], qo.at[0, 0, 1], load_sem.at[3]),
        pltpu.make_async_copy(tok_ref, own_tokens, load_sem.at[4]),
        pltpu.make_async_copy(gain_ref, gain_buf, load_sem.at[5]),
    ]
    for copy in loads:
        copy.start()
    far[...] = jnp.zeros_like(far)

    barrier = pltpu.get_barrier_semaphore()
    partners = [sibling]
    for off in (1, 2, 3):
        partners += [at_xy(0, off), at_xy(1, off)]
    partners += [along_z(1), along_z(-1)]
    for partner in partners:
        pl.semaphore_signal(barrier, inc=1, device_id=partner, device_id_type=MESH)
    pl.semaphore_wait(barrier, len(partners))

    def tell(n):
        for off in (2**n, -(2**n)):
            pl.semaphore_signal(ready_sem.at[n], inc=1, device_id=along_z(off), device_id_type=MESH)

    def hear(n):
        pl.semaphore_wait(ready_sem.at[n], 2)

    def part_of(s, half, first, second, sub=None):
        rows = BLK // 2
        start = half * rows
        if sub is not None:
            start, rows = start + sub * (rows // 2), rows // 2
        at = (second, first) if half == 0 else (first, second)
        if s == 0:
            return kv.at[(*at, pl.ds(start, rows))]
        return qo.at[(*at, s - 1, pl.ds(start, rows))]

    rest = pl.ds(1, 3)

    def send(src, dst, send_to, received, device):
        pltpu.make_async_remote_copy(
            src_ref=src, dst_ref=dst, send_sem=send_to, recv_sem=received, device_id=device, device_id_type=MESH
        ).start()

    def wait(ref, sem):
        pltpu.make_async_copy(ref, ref, sem).wait()

    def start_first(s):
        for off in (1, -1, 2):
            for half in (0, 1):
                to = slot_of(-off)
                send(part_of(s, half, 0, 0), part_of(s, half, to, 0), send_sem.at[s], first_sem.at[s, half, to], at_xy(half, off))

    def start_second(s):
        for half in (0, 1):
            for off in (1, -1):
                to = slot_of(-off)
                send(part_of(s, half, 0, 0), part_of(s, half, 0, to), send_sem.at[s], second_sem.at[s, half, 0, to], at_xy(1 - half, off))

    def wait_first(s, half, first):
        wait(part_of(s, half, first, 0), first_sem.at[s, half, first])

    def pass_second(s, half, first, index):
        for off in (1, -1):
            to = slot_of(-off)
            send(
                part_of(s, half, first, 0), part_of(s, half, first, to), send_sem.at[s],
                second_sem.at[s, half, index, to], at_xy(1 - half, off),
            )

    def wait_second(s, half, first, index, second):
        wait(part_of(s, half, first, second), second_sem.at[s, half, index, second])

    def pass_third(s, half, first, index, second):
        sub = 0 if OFFSETS[second] == -1 else 1
        send(
            part_of(s, half, first, second, sub), part_of(s, half, first, 3, sub), send_sem.at[s],
            third_sem.at[s, half, index, sub], at_xy(1 - half, -OFFSETS[second]),
        )

    def wait_third(s, half, first, index):
        for sub in (0, 1):
            wait(part_of(s, half, first, 3, sub), third_sem.at[s, half, index, sub])

    def pass_seconds(s):
        for half in (0, 1):
            for first in (1, 2, 3):
                wait_first(s, half, first)
            pass_second(s, half, rest, 1)

    def pass_thirds(s):
        for half in (0, 1):
            for second in (1, 2):
                wait_second(s, half, 0, 0, second)
                wait_second(s, half, rest, 1, second)
                pass_third(s, half, pl.ds(0, 4), 0, second)

    def sent(s):
        rows = pl.ds(0, BLK * 15 // 16)
        wait(kv.at[:, :, rows] if s == 0 else qo.at[:, :, 0, rows], send_sem.at[s])

    def block_at(a, b):
        return mod4(y + OFFSETS[a]) * SIDE + mod4(x + OFFSETS[b])

    def project(weights, acc, a):
        tokens = [x_buf[:, pl.ds(pl.multiple_of(block_at(a, b) * BLK, BLK), BLK)] for b in range(4)]
        term = jnp.dot(
            jnp.concatenate(tokens, axis=1), weights.reshape(SIDE * BLK, weights.shape[-1]), preferred_element_type=F32
        )
        if a == 0:
            acc[...] = term
        else:
            acc[...] += term

    loads[0].wait()
    loads[1].wait()
    start_first(0)
    start_second(0)
    tokens_out = pltpu.make_async_remote_copy(
        src_ref=tok_ref, dst_ref=own_tokens,
        send_sem=pair_send.at[0], recv_sem=pair_recv.at[0], device_id=sibling, device_id_type=MESH,
    )
    tokens_out.start()
    tell(0)
    for first in (1, 2, 3):
        for half in (0, 1):
            wait_first(0, half, first)
            pass_second(0, half, first, first)
    hear(0)
    tell(1)
    loads[2].wait()
    loads[3].wait()
    start_first(1)
    for half in (0, 1):
        for second in (1, 2):
            wait_second(0, half, 0, 0, second)
            pass_third(0, half, 0, 0, second)
    start_second(1)
    for half in (0, 1):
        for second in (1, 2):
            for first in (1, 2, 3):
                wait_second(0, half, first, first, second)
            pass_third(0, half, rest, 1, second)
    hear(1)
    tell(2)
    pass_seconds(1)
    start_first(2)
    start_second(2)
    hear(2)
    loads[4].wait()
    loads[5].wait()
    tokens_out.wait()

    for a in range(4):
        if a < 2:
            wait_third(0, 1, rest if a else 0, a)
        elif a == 3:
            wait_third(0, 0, 0, 0)
            wait_third(0, 0, rest, 1)
        project(kv[a], kv_acc, a)
    keys_in = kv_acc[:, :HEAD]
    k_act[...] = (keys_in / (1.0 + jnp.exp(-keys_in))).astype(BF16)
    v_act[...] = kv_acc[:, HEAD:].astype(BF16)
    for b in (0, 1):
        rows = pl.ds(b * TOK, TOK)
        state[b] = lax.dot_general(
            k_act[rows], v_act[rows], (((0,), (0,)), ((), ())), preferred_element_type=F32
        )
    near[mem] = (state[0] + state[1]).astype(BF16)

    for off in (1, 2, 3):
        send(near.at[mem], near.at[mem], scan_send.at[off - 1], near_sem.at[mem], at_z(grp, mod4(mem + off)))
    pass_thirds(1)
    pass_seconds(2)

    def send_wo(n, rows, columns):
        send(qo.at[rows, columns, 1], wo_pair.at[rows, columns], pair_send.at[1 + n], wo_recv.at[n], sibling)

    inner = pl.ds(0, 3)
    shares = [(inner, inner), (inner, 3), (3, pl.ds(0, 4))]
    for off in (1, 2, 3):
        m = mod4(mem + off)
        wait(near.at[m], near_sem.at[m])
    all_near = [near[m].astype(F32) for m in range(GROUP)]
    total[...] = (all_near[0] + all_near[1] + all_near[2] + all_near[3]).astype(BF16)

    targets = [(2, 3, 0), (2, 0, 3), (2, 3, 1), (2, 0, 2), (1, None, None), (3, None, None)]

    def sends_total(off, member):
        inside = grp + off < GROUPS
        return inside if member is None else jnp.logical_and(inside, mem == member)

    for n, (off, member, target) in enumerate(targets):

        @pl.when(sends_total(off, member))
        def _():
            pltpu.make_async_remote_copy(
                src_ref=total, dst_ref=far.at[grp], send_sem=scan_send.at[3 + n], recv_sem=far_sem.at[grp],
                device_id=at_z(grp + off, mem if target is None else target), device_id_type=MESH,
            ).start()

    prefix = jnp.zeros((HEAD, HEAD), F32)
    for m in range(GROUP - 1):
        prefix = prefix + jnp.where(m < mem, all_near[m], 0.0)

    for half in (0, 1):
        wait_third(1, half, pl.ds(0, 4), 0)
    for a in range(4):
        project(qo[a, :, 0], q_act, a)
    pass_thirds(2)
    send_wo(0, *shares[0])
    queries = q_act[...]
    q_act[...] = queries / (1.0 + jnp.exp(-queries))
    causal = lax.broadcasted_iota(jnp.int32, (TOK, TOK), 0) >= lax.broadcasted_iota(jnp.int32, (TOK, TOK), 1)
    for b in (0, 1):
        rows = pl.ds(b * TOK, TOK)
        scores = lax.dot_general(
            q_act[rows].astype(BF16), k_act[rows], (((1,), (1,)), ((), ())), preferred_element_type=F32
        )
        scores = jnp.where(causal, scores, 0.0).astype(BF16)
        intra[rows] = jnp.dot(scores, v_act[rows], preferred_element_type=F32)
    for g in range(GROUPS - 1):

        @pl.when(g < grp)
        def _():
            wait(far.at[g], far_sem.at[g])

        prefix = prefix + jnp.where(g < grp, far[g].astype(F32), 0.0)

    gain = gain_buf[pl.ds(core, 1), :]

    def normed(b):
        rows = pl.ds(pl.multiple_of(b * TOK, TOK), TOK)
        before = prefix + jnp.where(b == 1, state[0], 0.0)
        attended = intra[rows] + jnp.dot(
            q_act[rows].astype(BF16), before.astype(BF16), preferred_element_type=F32
        )
        meansq = jnp.mean(attended * attended, axis=-1, keepdims=True)
        return (attended * lax.rsqrt(meansq + 1e-06) * gain).astype(BF16)

    nrm_out[...] = normed(1 - core)
    nrm_copy = pltpu.make_async_remote_copy(
        src_ref=nrm_out, dst_ref=nrm.at[core], send_sem=pair_send.at[4], recv_sem=pair_recv.at[1],
        device_id=sibling, device_id_type=MESH,
    )
    nrm_copy.start()
    nrm[core] = normed(core)
    for half in (0, 1):
        wait_third(2, half, pl.ds(0, 4), 0)
    for n in (1, 2):
        send_wo(n, *shares[n])
    nrm_copy.wait()
    lhs = jnp.concatenate([nrm[0], nrm[1]], axis=1)
    stores = []
    order = [(a, b) for a in range(3) for b in range(3)] + [(a, 3) for a in range(3)] + [(3, b) for b in range(4)]
    for n, (a, b) in enumerate(order):
        if n in (0, 9, 12):
            share = (0, 9, 12).index(n)
            wait(wo_pair.at[shares[share]], wo_recv.at[share])
        block = block_at(a, b)
        columns = pl.ds(pl.multiple_of(block * BLK, BLK), BLK)
        own, other = qo[a, b, 1], wo_pair[a, b]
        weights = jnp.concatenate([jnp.where(core == 0, own, other), jnp.where(core == 0, other, own)], axis=1)
        out_buf[:, columns] = jnp.dot(lhs, weights, preferred_element_type=F32).astype(BF16)
        copy = pltpu.make_async_copy(out_buf.at[:, columns], out_ref.at[:, columns], store_sem.at[n])
        copy.start()
        stores.append(copy)
    for s in range(3):
        sent(s)
    for off in (1, 2, 3):
        wait(near.at[0], scan_send.at[off - 1])
    for n, share in enumerate(shares):
        wait(wo_pair.at[share], pair_send.at[1 + n])
    for n, (off, member, _) in enumerate(targets):

        @pl.when(sends_total(off, member))
        def _():
            wait(total, scan_send.at[3 + n])

    for copy in stores:
        copy.wait()


def shards(tokens, w_qkv, norm_gain, w_out):
    hbm = pl.BlockSpec(memory_space=pl.ANY)
    dma = pltpu.SemaphoreType.DMA
    width = tokens.shape[2]
    out = pl.pallas_call(
        kernel,
        out_shape=jax.ShapeDtypeStruct((TOK, width), BF16),
        in_specs=[hbm] * 4,
        out_specs=hbm,
        scratch_shapes=[
            pltpu.VMEM((2 * TOK, width), BF16),
            pltpu.VMEM((SIDE, SIDE, BLK, 2 * HEAD), BF16),
            pltpu.VMEM((SIDE, SIDE, 2, BLK, HEAD), BF16),
            pltpu.VMEM((SIDE, SIDE, BLK, HEAD), BF16),
            pltpu.VMEM((2 * TOK, HEAD), BF16),
            pltpu.VMEM((2 * TOK, HEAD), BF16),
            pltpu.VMEM((2 * TOK, HEAD), F32),
            pltpu.VMEM((GROUP, HEAD, HEAD), BF16),
            pltpu.VMEM((GROUPS, HEAD, HEAD), BF16),
            pltpu.VMEM((HEAD, HEAD), BF16),
            pltpu.VMEM((2, TOK, HEAD), BF16),
            pltpu.VMEM((TOK, HEAD), BF16),
            pltpu.VMEM((TOK, width), BF16),
            pltpu.VMEM((2, HEAD), F32),
            pltpu.VMEM((2 * TOK, 2 * HEAD), F32),
            pltpu.VMEM((2 * TOK, HEAD), F32),
            pltpu.VMEM((2, HEAD, HEAD), F32),
            dma((6,)),
            dma((3,)),
            dma((3, 2, 4)),
            dma((3, 2, 4, 3)),
            dma((3, 2, 2, 2)),
            dma((9,)),
            dma((GROUP,)),
            dma((GROUPS,)),
            dma((5,)),
            dma((2,)),
            dma((3,)),
            dma((16,)),
            pltpu.SemaphoreType.REGULAR((3,)),
        ],
        compiler_params=pltpu.CompilerParams(
            collective_id=0, has_side_effects=True, vmem_limit_bytes=48 * 1024 * 1024
        ),
        name="attention_layer",
    )(*(pltpu.with_memory_space_constraint(a, pltpu.HBM) for a in (tokens[0], w_qkv, norm_gain.reshape(2, HEAD), w_out)))
    return out[None]


def solution(mesh):
    return jax.shard_map(
        shards,
        mesh=mesh,
        in_specs=(P("dp", "seq", None), P("dp", None), P(), P(None, "dp")),
        out_specs=P("dp", "seq", None),
        check_vma=False,
    )
```

```python
import functools

import jax
import jax.numpy as jnp
from jax import lax
from jax.experimental import pallas as pl
from jax.experimental.pallas import tpu as pltpu
from jax.sharding import PartitionSpec as P

MESH = pl.DeviceIdType.MESH
BF16, F32 = jnp.bfloat16, jnp.float32
HEAD = 128
SIDE = 4
GROUP = 4
GROUPS = 4
TOK = 256
BLK = 256


OFFSETS = (0, 1, -1, 2)


def slot_of(off):
    return OFFSETS.index(2 if off in (2, -2) else off)


def mod4(value):
    return lax.rem(value + 8, 4)


def kernel(
    tok_ref, w_ref, gain_ref, wo_ref, out_ref,
    x_buf, kv, qo, wo_pair, k_act, v_act, intra, near, far, total, nrm, nrm_out, gain_buf,
    kv_acc, q_act, state,
    load_sem, send_sem, first_sem, second_sem, third_sem, scan_send, near_sem, far_sem, pair_send, pair_recv, wo_recv,
    ready_sem,
):
    dp, seq = lax.axis_index("dp"), lax.axis_index("seq")
    y, x = lax.div(dp, SIDE), lax.rem(dp, SIDE)
    z, core = lax.div(seq, 2), lax.rem(seq, 2)
    grp, mem = lax.div(z, GROUP), lax.rem(z, GROUP)
    sibling = (dp, z * 2 + (1 - core))
    lane = pl.multiple_of(core * HEAD, HEAD)

    def at_xy(axis, off):
        if axis == 0:
            return (y * SIDE + mod4(x + off), seq)
        return (mod4(y + off) * SIDE + x, seq)

    def at_z(g, m):
        return (dp, (g * GROUP + m) * 2 + core)

    def along_z(off):
        return (dp, lax.rem(z + off + 16, 16) * 2 + core)

    own_tokens = x_buf.at[pl.ds(pl.multiple_of(core * TOK, TOK), TOK)]
    loads = [
        pltpu.make_async_copy(w_ref.at[:, pl.ds(2 * HEAD + lane, HEAD)], kv.at[0, 0, :, pl.ds(0, HEAD)], load_sem.at[0]),
        pltpu.make_async_copy(w_ref.at[:, pl.ds(4 * HEAD + lane, HEAD)], kv.at[0, 0, :, pl.ds(HEAD, HEAD)], load_sem.at[1]),
        pltpu.make_async_copy(w_ref.at[:, pl.ds(lane, HEAD)], qo.at[0, 0, 0], load_sem.at[2]),
        pltpu.make_async_copy(wo_ref.at[:, pl.ds(lane, HEAD)], qo.at[0, 0, 1], load_sem.at[3]),
        pltpu.make_async_copy(tok_ref, own_tokens, load_sem.at[4]),
        pltpu.make_async_copy(gain_ref, gain_buf, load_sem.at[5]),
    ]
    for copy in loads:
        copy.start()
    far[...] = jnp.zeros_like(far)

    barrier = pltpu.get_barrier_semaphore()
    partners = [sibling]
    for off in (1, 2, 3):
        partners += [at_xy(0, off), at_xy(1, off)]
    partners += [along_z(1), along_z(-1)]
    for partner in partners:
        pl.semaphore_signal(barrier, inc=1, device_id=partner, device_id_type=MESH)
    pl.semaphore_wait(barrier, len(partners))

    def tell(n):
        for off in (2**n, -(2**n)):
            pl.semaphore_signal(ready_sem.at[n], inc=1, device_id=along_z(off), device_id_type=MESH)

    def hear(n):
        pl.semaphore_wait(ready_sem.at[n], 2)

    def part_of(s, half, first, second, sub=None):
        rows = BLK // 2
        start = half * rows
        if sub is not None:
            start, rows = start + sub * (rows // 2), rows // 2
        at = (second, first) if half == 0 else (first, second)
        if s == 0:
            return kv.at[(*at, pl.ds(start, rows))]
        return qo.at[(*at, s - 1, pl.ds(start, rows))]

    rest = pl.ds(1, 3)

    def send(src, dst, send_to, received, device):
        pltpu.make_async_remote_copy(
            src_ref=src, dst_ref=dst, send_sem=send_to, recv_sem=received, device_id=device, device_id_type=MESH
        ).start()

    def wait(ref, sem):
        pltpu.make_async_copy(ref, ref, sem).wait()

    def around(s):
        return (2, 1, -1) if s == 2 else (1, -1)

    def start_first(s):
        for off in (1, -1, 2):
            for half in (0, 1):
                to = slot_of(-off)
                send(part_of(s, half, 0, 0), part_of(s, half, to, 0), send_sem.at[s], first_sem.at[s, half, to], at_xy(half, off))

    def start_second(s):
        for half in (0, 1):
            for off in around(s):
                to = slot_of(-off)
                send(part_of(s, half, 0, 0), part_of(s, half, 0, to), send_sem.at[s], second_sem.at[s, half, 0, to], at_xy(1 - half, off))

    def wait_first(s, half, first):
        wait(part_of(s, half, first, 0), first_sem.at[s, half, first])

    def pass_second(s, half, first, index):
        for off in around(s):
            to = slot_of(-off)
            send(
                part_of(s, half, first, 0), part_of(s, half, first, to), send_sem.at[s],
                second_sem.at[s, half, index, to], at_xy(1 - half, off),
            )

    def wait_second(s, half, first, index, second):
        wait(part_of(s, half, first, second), second_sem.at[s, half, index, second])

    def pass_third(s, half, first, index, second):
        sub = 0 if OFFSETS[second] == -1 else 1
        send(
            part_of(s, half, first, second, sub), part_of(s, half, first, 3, sub), send_sem.at[s],
            third_sem.at[s, half, index, sub], at_xy(1 - half, -OFFSETS[second]),
        )

    def wait_third(s, half, first, index):
        for sub in (0, 1):
            wait(part_of(s, half, first, 3, sub), third_sem.at[s, half, index, sub])

    def pass_seconds(s):
        for half in (0, 1):
            for first in (1, 2, 3):
                wait_first(s, half, first)
            pass_second(s, half, rest, 1)

    def pass_thirds(s):
        for half in (0, 1):
            for second in (1, 2):
                wait_second(s, half, 0, 0, second)
                wait_second(s, half, rest, 1, second)
                pass_third(s, half, pl.ds(0, 4), 0, second)

    def sent(s):
        rows = pl.ds(0, BLK * 15 // 16)
        wait(kv.at[:, :, rows] if s == 0 else qo.at[:, :, 0, rows], send_sem.at[s])

    def block_at(a, b):
        return mod4(y + OFFSETS[a]) * SIDE + mod4(x + OFFSETS[b])

    def project(weights, acc, slots, add):
        tokens = [x_buf[:, pl.ds(pl.multiple_of(block_at(a, b) * BLK, BLK), BLK)] for a, b in slots]
        term = jnp.dot(
            jnp.concatenate(tokens, axis=1), weights.reshape(len(slots) * BLK, weights.shape[-1]), preferred_element_type=F32
        )
        acc[...] = acc[...] + term if add else term

    loads[0].wait()
    loads[1].wait()
    start_first(0)
    start_second(0)
    tokens_out = pltpu.make_async_remote_copy(
        src_ref=tok_ref, dst_ref=own_tokens,
        send_sem=pair_send.at[0], recv_sem=pair_recv.at[0], device_id=sibling, device_id_type=MESH,
    )
    tokens_out.start()
    tell(0)
    for first in (1, 2, 3):
        for half in (0, 1):
            wait_first(0, half, first)
            pass_second(0, half, first, first)
    hear(0)
    tell(1)
    loads[2].wait()
    loads[3].wait()
    start_first(1)
    for half in (0, 1):
        for second in (1, 2):
            wait_second(0, half, 0, 0, second)
            pass_third(0, half, 0, 0, second)
    start_second(1)
    for half in (0, 1):
        for second in (1, 2):
            for first in (1, 2, 3):
                wait_second(0, half, first, first, second)
            pass_third(0, half, rest, 1, second)
    hear(1)
    tell(2)
    pass_seconds(1)
    start_first(2)
    start_second(2)
    hear(2)
    loads[4].wait()
    loads[5].wait()
    tokens_out.wait()

    for a in range(3):
        project(kv[a, 0:3], kv_acc, [(a, b) for b in range(3)], a > 0)
    wait_third(0, 1, 0, 0)
    wait_third(0, 1, rest, 1)
    project(kv[0:3, 3], kv_acc, [(a, 3) for a in range(3)], True)
    wait_third(0, 0, 0, 0)
    wait_third(0, 0, rest, 1)
    project(kv[3], kv_acc, [(3, b) for b in range(4)], True)
    keys_in = kv_acc[:, :HEAD]
    k_act[...] = (keys_in / (1.0 + jnp.exp(-keys_in))).astype(BF16)
    v_act[...] = kv_acc[:, HEAD:].astype(BF16)
    for b in (0, 1):
        rows = pl.ds(b * TOK, TOK)
        state[b] = lax.dot_general(
            k_act[rows], v_act[rows], (((0,), (0,)), ((), ())), preferred_element_type=F32
        )
    near[mem] = (state[0] + state[1]).astype(BF16)

    for off in (1, 2, 3):
        send(near.at[mem], near.at[mem], scan_send.at[off - 1], near_sem.at[mem], at_z(grp, mod4(mem + off)))
    pass_thirds(1)
    pass_seconds(2)

    def send_wo(n, rows, columns):
        send(qo.at[rows, columns, 1], wo_pair.at[rows, columns], pair_send.at[1 + n], wo_recv.at[n], sibling)

    inner = pl.ds(0, 3)
    shares = [(inner, inner), (inner, 3), (3, pl.ds(0, 4))]
    for off in (1, 2, 3):
        m = mod4(mem + off)
        wait(near.at[m], near_sem.at[m])
    all_near = [near[m].astype(F32) for m in range(GROUP)]
    total[...] = (all_near[0] + all_near[1] + all_near[2] + all_near[3]).astype(BF16)

    targets = [(2, 3, 0), (2, 0, 3), (2, 3, 1), (2, 0, 2), (1, None, None), (3, None, None)]

    def sends_total(off, member):
        inside = grp + off < GROUPS
        return inside if member is None else jnp.logical_and(inside, mem == member)

    for n, (off, member, target) in enumerate(targets):

        @pl.when(sends_total(off, member))
        def _():
            pltpu.make_async_remote_copy(
                src_ref=total, dst_ref=far.at[grp], send_sem=scan_send.at[3 + n], recv_sem=far_sem.at[grp],
                device_id=at_z(grp + off, mem if target is None else target), device_id_type=MESH,
            ).start()

    prefix = jnp.zeros((HEAD, HEAD), F32)
    for m in range(GROUP - 1):
        prefix = prefix + jnp.where(m < mem, all_near[m], 0.0)

    for half in (0, 1):
        wait_third(1, half, pl.ds(0, 4), 0)
    for a in range(4):
        project(qo[a, :, 0], q_act, [(a, b) for b in range(4)], a > 0)
    for half in (0, 1):
        for second in (1, 2):
            wait_second(2, half, 0, 0, second)
            wait_second(2, half, rest, 1, second)
    send_wo(0, *shares[0])
    queries = q_act[...]
    q_act[...] = queries / (1.0 + jnp.exp(-queries))
    causal = lax.broadcasted_iota(jnp.int32, (TOK, TOK), 0) >= lax.broadcasted_iota(jnp.int32, (TOK, TOK), 1)
    for b in (0, 1):
        rows = pl.ds(b * TOK, TOK)
        scores = lax.dot_general(
            q_act[rows].astype(BF16), k_act[rows], (((1,), (1,)), ((), ())), preferred_element_type=F32
        )
        scores = jnp.where(causal, scores, 0.0).astype(BF16)
        intra[rows] = jnp.dot(scores, v_act[rows], preferred_element_type=F32)
    for g in range(GROUPS - 1):

        @pl.when(g < grp)
        def _():
            wait(far.at[g], far_sem.at[g])

        prefix = prefix + jnp.where(g < grp, far[g].astype(F32), 0.0)

    gain = gain_buf[pl.ds(core, 1), :]

    def normed(b):
        rows = pl.ds(pl.multiple_of(b * TOK, TOK), TOK)
        before = prefix + jnp.where(b == 1, state[0], 0.0)
        attended = intra[rows] + jnp.dot(
            q_act[rows].astype(BF16), before.astype(BF16), preferred_element_type=F32
        )
        meansq = jnp.mean(attended * attended, axis=-1, keepdims=True)
        return (attended * lax.rsqrt(meansq + 1e-06) * gain).astype(BF16)

    nrm_out[...] = normed(1 - core)
    nrm_copy = pltpu.make_async_remote_copy(
        src_ref=nrm_out, dst_ref=nrm.at[core], send_sem=pair_send.at[4], recv_sem=pair_recv.at[1],
        device_id=sibling, device_id_type=MESH,
    )
    nrm_copy.start()
    nrm[core] = normed(core)
    for half in (0, 1):
        wait_second(2, half, 0, 0, 3)
        wait_second(2, half, rest, 1, 3)
    for n in (1, 2):
        send_wo(n, *shares[n])
    nrm_copy.wait()
    lhs = jnp.concatenate([nrm[0], nrm[1]], axis=1)
    order = [(a, b) for a in range(3) for b in range(3)] + [(a, 3) for a in range(3)] + [(3, b) for b in range(4)]
    for n, (a, b) in enumerate(order):
        if n in (0, 9, 12):
            share = (0, 9, 12).index(n)
            wait(wo_pair.at[shares[share]], wo_recv.at[share])
        block = block_at(a, b)
        columns = pl.ds(pl.multiple_of(block * BLK, BLK), BLK)
        own, other = qo[a, b, 1], wo_pair[a, b]
        weights = jnp.concatenate([jnp.where(core == 0, own, other), jnp.where(core == 0, other, own)], axis=1)
        out_ref[:, columns] = jnp.dot(lhs, weights, preferred_element_type=F32).astype(BF16)
    for s in range(3):
        sent(s)
    for off in (1, 2, 3):
        wait(near.at[0], scan_send.at[off - 1])
    for n, share in enumerate(shares):
        wait(wo_pair.at[share], pair_send.at[1 + n])
    for n, (off, member, _) in enumerate(targets):

        @pl.when(sends_total(off, member))
        def _():
            wait(total, scan_send.at[3 + n])


def shards(tokens, w_qkv, norm_gain, w_out):
    hbm = pl.BlockSpec(memory_space=pl.ANY)
    dma = pltpu.SemaphoreType.DMA
    width = tokens.shape[2]
    out = pl.pallas_call(
        kernel,
        out_shape=jax.ShapeDtypeStruct((TOK, width), BF16),
        in_specs=[hbm] * 4,
        out_specs=pl.BlockSpec(memory_space=pltpu.VMEM),
        scratch_shapes=[
            pltpu.VMEM((2 * TOK, width), BF16),
            pltpu.VMEM((SIDE, SIDE, BLK, 2 * HEAD), BF16),
            pltpu.VMEM((SIDE, SIDE, 2, BLK, HEAD), BF16),
            pltpu.VMEM((SIDE, SIDE, BLK, HEAD), BF16),
            pltpu.VMEM((2 * TOK, HEAD), BF16),
            pltpu.VMEM((2 * TOK, HEAD), BF16),
            pltpu.VMEM((2 * TOK, HEAD), F32),
            pltpu.VMEM((GROUP, HEAD, HEAD), BF16),
            pltpu.VMEM((GROUPS, HEAD, HEAD), BF16),
            pltpu.VMEM((HEAD, HEAD), BF16),
            pltpu.VMEM((2, TOK, HEAD), BF16),
            pltpu.VMEM((TOK, HEAD), BF16),
            pltpu.VMEM((2, HEAD), F32),
            pltpu.VMEM((2 * TOK, 2 * HEAD), F32),
            pltpu.VMEM((2 * TOK, HEAD), F32),
            pltpu.VMEM((2, HEAD, HEAD), F32),
            dma((6,)),
            dma((3,)),
            dma((3, 2, 4)),
            dma((3, 2, 4, 4)),
            dma((3, 2, 2, 2)),
            dma((9,)),
            dma((GROUP,)),
            dma((GROUPS,)),
            dma((5,)),
            dma((2,)),
            dma((3,)),
            pltpu.SemaphoreType.REGULAR((3,)),
        ],
        compiler_params=pltpu.CompilerParams(
            collective_id=0, has_side_effects=True, vmem_limit_bytes=48 * 1024 * 1024
        ),
        name="attention_layer",
    )(*(pltpu.with_memory_space_constraint(a, pltpu.HBM) for a in (tokens[0], w_qkv, norm_gain.reshape(2, HEAD), w_out)))
    return out[None]


def solution(mesh):
    return jax.shard_map(
        shards,
        mesh=mesh,
        in_specs=(P("dp", "seq", None), P("dp", None), P(), P(None, "dp")),
        out_specs=P("dp", "seq", None),
        check_vma=False,
    )
```

```python
import functools

import jax
import jax.numpy as jnp
from jax import lax
from jax.experimental import pallas as pl
from jax.experimental.pallas import tpu as pltpu
from jax.sharding import PartitionSpec as P

MESH = pl.DeviceIdType.MESH
BF16, F32 = jnp.bfloat16, jnp.float32
HEAD = 128
SIDE = 4
GROUP = 4
GROUPS = 4
TOK = 256
BLK = 256


OFFSETS = (0, 1, -1, 2)


def slot_of(off):
    return OFFSETS.index(2 if off in (2, -2) else off)


def mod4(value):
    return lax.rem(value + 8, 4)


def kernel(
    tok_ref, w_ref, gain_ref, wo_ref, out_ref,
    x_buf, kv, qo, wo_pair, k_act, v_act, intra, near, far, total, nrm, nrm_out, gain_buf,
    kv_acc, q_act, state,
    load_sem, send_sem, first_sem, second_sem, third_sem, scan_send, near_sem, far_sem, pair_send, pair_recv, wo_recv,
    ready_sem,
):
    dp, seq = lax.axis_index("dp"), lax.axis_index("seq")
    y, x = lax.div(dp, SIDE), lax.rem(dp, SIDE)
    z, core = lax.div(seq, 2), lax.rem(seq, 2)
    grp, mem = lax.div(z, GROUP), lax.rem(z, GROUP)
    sibling = (dp, z * 2 + (1 - core))
    lane = pl.multiple_of(core * HEAD, HEAD)

    def at_xy(axis, off):
        if axis == 0:
            return (y * SIDE + mod4(x + off), seq)
        return (mod4(y + off) * SIDE + x, seq)

    def at_z(g, m):
        return (dp, (g * GROUP + m) * 2 + core)

    def along_z(off):
        return (dp, lax.rem(z + off + 16, 16) * 2 + core)

    own_tokens = x_buf.at[pl.ds(pl.multiple_of(core * TOK, TOK), TOK)]
    loads = [
        pltpu.make_async_copy(w_ref.at[:, pl.ds(2 * HEAD + lane, HEAD)], kv.at[0, 0, :, pl.ds(0, HEAD)], load_sem.at[0]),
        pltpu.make_async_copy(w_ref.at[:, pl.ds(4 * HEAD + lane, HEAD)], kv.at[0, 0, :, pl.ds(HEAD, HEAD)], load_sem.at[1]),
        pltpu.make_async_copy(w_ref.at[:, pl.ds(lane, HEAD)], qo.at[0, 0, 0], load_sem.at[2]),
        pltpu.make_async_copy(wo_ref.at[:, pl.ds(lane, HEAD)], qo.at[0, 0, 1], load_sem.at[3]),
        pltpu.make_async_copy(tok_ref, own_tokens, load_sem.at[4]),
        pltpu.make_async_copy(gain_ref, gain_buf, load_sem.at[5]),
    ]
    for copy in loads:
        copy.start()
    far[...] = jnp.zeros_like(far)

    barrier = pltpu.get_barrier_semaphore()
    partners = [sibling]
    for off in (1, 2, 3):
        partners += [at_xy(0, off), at_xy(1, off)]
    partners += [along_z(1), along_z(-1)]
    for partner in partners:
        pl.semaphore_signal(barrier, inc=1, device_id=partner, device_id_type=MESH)
    pl.semaphore_wait(barrier, len(partners))

    def tell(n):
        for off in (2**n, -(2**n)):
            pl.semaphore_signal(ready_sem.at[n], inc=1, device_id=along_z(off), device_id_type=MESH)

    def hear(n):
        pl.semaphore_wait(ready_sem.at[n], 2)

    def part_of(s, half, first, second, sub=None):
        rows = BLK // 2
        start = half * rows
        if sub is not None:
            start, rows = start + sub * (rows // 2), rows // 2
        at = (second, first) if half == 0 else (first, second)
        if s == 0:
            return kv.at[(*at, pl.ds(start, rows))]
        return qo.at[(*at, s - 1, pl.ds(start, rows))]

    rest = pl.ds(1, 3)

    def send(src, dst, send_to, received, device):
        pltpu.make_async_remote_copy(
            src_ref=src, dst_ref=dst, send_sem=send_to, recv_sem=received, device_id=device, device_id_type=MESH
        ).start()

    def wait(ref, sem):
        pltpu.make_async_copy(ref, ref, sem).wait()

    def around(s):
        return (2, 1, -1) if s == 2 else (1, -1)

    def start_first(s):
        for off in (1, -1, 2):
            for half in (0, 1):
                to = slot_of(-off)
                send(part_of(s, half, 0, 0), part_of(s, half, to, 0), send_sem.at[s], first_sem.at[s, half, to], at_xy(half, off))

    def start_second(s):
        for half in (0, 1):
            for off in around(s):
                to = slot_of(-off)
                send(part_of(s, half, 0, 0), part_of(s, half, 0, to), send_sem.at[s], second_sem.at[s, half, 0, to], at_xy(1 - half, off))

    def wait_first(s, half, first):
        wait(part_of(s, half, first, 0), first_sem.at[s, half, first])

    def pass_second(s, half, first, index):
        for off in around(s):
            to = slot_of(-off)
            send(
                part_of(s, half, first, 0), part_of(s, half, first, to), send_sem.at[s],
                second_sem.at[s, half, index, to], at_xy(1 - half, off),
            )

    def wait_second(s, half, first, index, second):
        wait(part_of(s, half, first, second), second_sem.at[s, half, index, second])

    def pass_third(s, half, first, index, second):
        sub = 0 if OFFSETS[second] == -1 else 1
        send(
            part_of(s, half, first, second, sub), part_of(s, half, first, 3, sub), send_sem.at[s],
            third_sem.at[s, half, index, sub], at_xy(1 - half, -OFFSETS[second]),
        )

    def wait_third(s, half, first, index):
        for sub in (0, 1):
            wait(part_of(s, half, first, 3, sub), third_sem.at[s, half, index, sub])

    def pass_seconds(s):
        for half in (0, 1):
            for first in (1, 2, 3):
                wait_first(s, half, first)
            pass_second(s, half, rest, 1)

    def pass_thirds(s):
        for half in (0, 1):
            for second in (1, 2):
                wait_second(s, half, 0, 0, second)
                wait_second(s, half, rest, 1, second)
                pass_third(s, half, pl.ds(0, 4), 0, second)

    def sent(s):
        rows = pl.ds(0, BLK * 15 // 16)
        wait(kv.at[:, :, rows] if s == 0 else qo.at[:, :, 0, rows], send_sem.at[s])

    def block_at(a, b):
        return mod4(y + OFFSETS[a]) * SIDE + mod4(x + OFFSETS[b])

    def project(weights, acc, slots, add):
        tokens = [x_buf[:, pl.ds(pl.multiple_of(block_at(a, b) * BLK, BLK), BLK)] for a, b in slots]
        term = jnp.dot(
            jnp.concatenate(tokens, axis=1), weights.reshape(len(slots) * BLK, weights.shape[-1]), preferred_element_type=F32
        )
        acc[...] = acc[...] + term if add else term

    loads[0].wait()
    loads[1].wait()
    start_first(0)
    start_second(0)
    tokens_out = pltpu.make_async_remote_copy(
        src_ref=tok_ref, dst_ref=own_tokens,
        send_sem=pair_send.at[0], recv_sem=pair_recv.at[0], device_id=sibling, device_id_type=MESH,
    )
    tokens_out.start()
    tell(0)
    for first in (1, 2, 3):
        for half in (0, 1):
            wait_first(0, half, first)
            pass_second(0, half, first, first)
    hear(0)
    tell(1)
    loads[2].wait()
    loads[3].wait()
    start_first(1)
    for half in (0, 1):
        for second in (1, 2):
            wait_second(0, half, 0, 0, second)
            pass_third(0, half, 0, 0, second)
    start_second(1)
    for half in (0, 1):
        for second in (1, 2):
            for first in (1, 2, 3):
                wait_second(0, half, first, first, second)
            pass_third(0, half, rest, 1, second)
    hear(1)
    tell(2)
    pass_seconds(1)
    start_first(2)
    start_second(2)
    hear(2)
    loads[4].wait()
    loads[5].wait()
    tokens_out.wait()

    for a in range(3):
        project(kv[a, 0:3], kv_acc, [(a, b) for b in range(3)], a > 0)
    wait_third(0, 1, 0, 0)
    wait_third(0, 1, rest, 1)
    project(kv[0:3, 3], kv_acc, [(a, 3) for a in range(3)], True)
    wait_third(0, 0, 0, 0)
    wait_third(0, 0, rest, 1)
    project(kv[3], kv_acc, [(3, b) for b in range(4)], True)
    keys_in = kv_acc[:, :HEAD]
    k_act[...] = (keys_in / (1.0 + jnp.exp(-keys_in))).astype(BF16)
    v_act[...] = kv_acc[:, HEAD:].astype(BF16)
    for b in (0, 1):
        rows = pl.ds(b * TOK, TOK)
        state[b] = lax.dot_general(
            k_act[rows], v_act[rows], (((0,), (0,)), ((), ())), preferred_element_type=F32
        )
    near[mem] = (state[0] + state[1]).astype(BF16)

    for off in (1, 2, 3):
        send(near.at[mem], near.at[mem], scan_send.at[off - 1], near_sem.at[mem], at_z(grp, mod4(mem + off)))
    pass_thirds(1)
    pass_seconds(2)

    def send_wo(n, rows, columns):
        send(qo.at[rows, columns, 1], wo_pair.at[rows, columns], pair_send.at[1 + n], wo_recv.at[n], sibling)

    inner = pl.ds(0, 3)
    shares = [(inner, inner), (inner, 3), (3, pl.ds(0, 4))]
    for off in (1, 2, 3):
        m = mod4(mem + off)
        wait(near.at[m], near_sem.at[m])
    all_near = [near[m].astype(F32) for m in range(GROUP)]
    total[...] = (all_near[0] + all_near[1] + all_near[2] + all_near[3]).astype(BF16)

    targets = [(2, 3, 0), (2, 0, 3), (2, 3, 1), (2, 0, 2), (1, None, None), (3, None, None)]

    def sends_total(off, member):
        inside = grp + off < GROUPS
        return inside if member is None else jnp.logical_and(inside, mem == member)

    for n, (off, member, target) in enumerate(targets):

        @pl.when(sends_total(off, member))
        def _():
            pltpu.make_async_remote_copy(
                src_ref=total, dst_ref=far.at[grp], send_sem=scan_send.at[3 + n], recv_sem=far_sem.at[grp],
                device_id=at_z(grp + off, mem if target is None else target), device_id_type=MESH,
            ).start()

    prefix = jnp.zeros((HEAD, HEAD), F32)
    for m in range(GROUP - 1):
        prefix = prefix + jnp.where(m < mem, all_near[m], 0.0)

    for half in (0, 1):
        wait_third(1, half, pl.ds(0, 4), 0)
    for a in range(4):
        project(qo[a, :, 0], q_act, [(a, b) for b in range(4)], a > 0)
    queries = q_act[...]
    q_act[...] = queries / (1.0 + jnp.exp(-queries))
    causal = lax.broadcasted_iota(jnp.int32, (TOK, TOK), 0) >= lax.broadcasted_iota(jnp.int32, (TOK, TOK), 1)
    for b in (0, 1):
        rows = pl.ds(b * TOK, TOK)
        scores = lax.dot_general(
            q_act[rows].astype(BF16), k_act[rows], (((1,), (1,)), ((), ())), preferred_element_type=F32
        )
        scores = jnp.where(causal, scores, 0.0).astype(BF16)
        intra[rows] = jnp.dot(scores, v_act[rows], preferred_element_type=F32)
    for half in (0, 1):
        for second in (1, 2):
            wait_second(2, half, 0, 0, second)
            wait_second(2, half, rest, 1, second)
    send_wo(0, *shares[0])
    for g in range(GROUPS - 1):

        @pl.when(g < grp)
        def _():
            wait(far.at[g], far_sem.at[g])

        prefix = prefix + jnp.where(g < grp, far[g].astype(F32), 0.0)

    gain = gain_buf[pl.ds(core, 1), :]

    def normed(b):
        rows = pl.ds(pl.multiple_of(b * TOK, TOK), TOK)
        before = prefix + jnp.where(b == 1, state[0], 0.0)
        attended = intra[rows] + jnp.dot(
            q_act[rows].astype(BF16), before.astype(BF16), preferred_element_type=F32
        )
        meansq = jnp.mean(attended * attended, axis=-1, keepdims=True)
        return (attended * lax.rsqrt(meansq + 1e-06) * gain).astype(BF16)

    nrm_out[...] = normed(1 - core)
    nrm_copy = pltpu.make_async_remote_copy(
        src_ref=nrm_out, dst_ref=nrm.at[core], send_sem=pair_send.at[4], recv_sem=pair_recv.at[1],
        device_id=sibling, device_id_type=MESH,
    )
    nrm_copy.start()
    nrm[core] = normed(core)
    for half in (0, 1):
        wait_second(2, half, 0, 0, 3)
        wait_second(2, half, rest, 1, 3)
    for n in (1, 2):
        send_wo(n, *shares[n])
    nrm_copy.wait()
    lhs = jnp.concatenate([nrm[0], nrm[1]], axis=1)
    order = [(a, b) for a in range(3) for b in range(3)] + [(a, 3) for a in range(3)] + [(3, b) for b in range(4)]
    for n, (a, b) in enumerate(order):
        if n in (0, 9, 12):
            share = (0, 9, 12).index(n)
            wait(wo_pair.at[shares[share]], wo_recv.at[share])
        block = block_at(a, b)
        columns = pl.ds(pl.multiple_of(block * BLK, BLK), BLK)
        own, other = qo[a, b, 1], wo_pair[a, b]
        weights = jnp.concatenate([jnp.where(core == 0, own, other), jnp.where(core == 0, other, own)], axis=1)
        out_ref[:, columns] = jnp.dot(lhs, weights, preferred_element_type=F32).astype(BF16)
    for s in range(3):
        sent(s)
    for off in (1, 2, 3):
        wait(near.at[0], scan_send.at[off - 1])
    for n, share in enumerate(shares):
        wait(wo_pair.at[share], pair_send.at[1 + n])
    for n, (off, member, _) in enumerate(targets):

        @pl.when(sends_total(off, member))
        def _():
            wait(total, scan_send.at[3 + n])


def shards(tokens, w_qkv, norm_gain, w_out):
    hbm = pl.BlockSpec(memory_space=pl.ANY)
    dma = pltpu.SemaphoreType.DMA
    width = tokens.shape[2]
    out = pl.pallas_call(
        kernel,
        out_shape=jax.ShapeDtypeStruct((TOK, width), BF16),
        in_specs=[hbm] * 4,
        out_specs=pl.BlockSpec(memory_space=pltpu.VMEM),
        scratch_shapes=[
            pltpu.VMEM((2 * TOK, width), BF16),
            pltpu.VMEM((SIDE, SIDE, BLK, 2 * HEAD), BF16),
            pltpu.VMEM((SIDE, SIDE, 2, BLK, HEAD), BF16),
            pltpu.VMEM((SIDE, SIDE, BLK, HEAD), BF16),
            pltpu.VMEM((2 * TOK, HEAD), BF16),
            pltpu.VMEM((2 * TOK, HEAD), BF16),
            pltpu.VMEM((2 * TOK, HEAD), F32),
            pltpu.VMEM((GROUP, HEAD, HEAD), BF16),
            pltpu.VMEM((GROUPS, HEAD, HEAD), BF16),
            pltpu.VMEM((HEAD, HEAD), BF16),
            pltpu.VMEM((2, TOK, HEAD), BF16),
            pltpu.VMEM((TOK, HEAD), BF16),
            pltpu.VMEM((2, HEAD), F32),
            pltpu.VMEM((2 * TOK, 2 * HEAD), F32),
            pltpu.VMEM((2 * TOK, HEAD), F32),
            pltpu.VMEM((2, HEAD, HEAD), F32),
            dma((6,)),
            dma((3,)),
            dma((3, 2, 4)),
            dma((3, 2, 4, 4)),
            dma((3, 2, 2, 2)),
            dma((9,)),
            dma((GROUP,)),
            dma((GROUPS,)),
            dma((5,)),
            dma((2,)),
            dma((3,)),
            pltpu.SemaphoreType.REGULAR((3,)),
        ],
        compiler_params=pltpu.CompilerParams(
            collective_id=0, has_side_effects=True, vmem_limit_bytes=48 * 1024 * 1024
        ),
        name="attention_layer",
    )(*(pltpu.with_memory_space_constraint(a, pltpu.HBM) for a in (tokens[0], w_qkv, norm_gain.reshape(2, HEAD), w_out)))
    return out[None]


def solution(mesh):
    return jax.shard_map(
        shards,
        mesh=mesh,
        in_specs=(P("dp", "seq", None), P("dp", None), P(), P(None, "dp")),
        out_specs=P("dp", "seq", None),
        check_vma=False,
    )
```

```python
import functools

import jax
import jax.numpy as jnp
from jax import lax
from jax.experimental import pallas as pl
from jax.experimental.pallas import tpu as pltpu
from jax.sharding import PartitionSpec as P

MESH = pl.DeviceIdType.MESH
BF16, F32 = jnp.bfloat16, jnp.float32
HEAD = 128
SIDE = 4
GROUP = 4
GROUPS = 4
TOK = 256
BLK = 256


OFFSETS = (0, 1, -1, 2)


def slot_of(off):
    return OFFSETS.index(2 if off in (2, -2) else off)


def mod4(value):
    return lax.rem(value + 8, 4)


def kernel(
    tok_ref, w_ref, gain_ref, wo_ref, out_ref,
    x_buf, kv, qo, wo_pair, k_act, v_act, intra, near, far, total, nrm, nrm_out, gain_buf,
    kv_acc, q_act, state,
    load_sem, send_sem, first_sem, second_sem, third_sem, scan_send, near_sem, far_sem, pair_send, pair_recv, wo_recv,
    ready_sem,
):
    dp, seq = lax.axis_index("dp"), lax.axis_index("seq")
    y, x = lax.div(dp, SIDE), lax.rem(dp, SIDE)
    z, core = lax.div(seq, 2), lax.rem(seq, 2)
    grp, mem = lax.div(z, GROUP), lax.rem(z, GROUP)
    sibling = (dp, z * 2 + (1 - core))
    lane = pl.multiple_of(core * HEAD, HEAD)

    def at_xy(axis, off):
        if axis == 0:
            return (y * SIDE + mod4(x + off), seq)
        return (mod4(y + off) * SIDE + x, seq)

    def at_z(g, m):
        return (dp, (g * GROUP + m) * 2 + core)

    def along_z(off):
        return (dp, lax.rem(z + off + 16, 16) * 2 + core)

    own_tokens = x_buf.at[pl.ds(pl.multiple_of(core * TOK, TOK), TOK)]
    loads = [
        pltpu.make_async_copy(w_ref.at[:, pl.ds(2 * HEAD + lane, HEAD)], kv.at[0, 0, :, pl.ds(0, HEAD)], load_sem.at[0]),
        pltpu.make_async_copy(w_ref.at[:, pl.ds(4 * HEAD + lane, HEAD)], kv.at[0, 0, :, pl.ds(HEAD, HEAD)], load_sem.at[1]),
        pltpu.make_async_copy(w_ref.at[:, pl.ds(lane, HEAD)], qo.at[0, 0, 0], load_sem.at[2]),
        pltpu.make_async_copy(wo_ref.at[:, pl.ds(lane, HEAD)], qo.at[0, 0, 1], load_sem.at[3]),
        pltpu.make_async_copy(tok_ref, own_tokens, load_sem.at[4]),
        pltpu.make_async_copy(gain_ref, gain_buf, load_sem.at[5]),
    ]
    for copy in loads[:4] + loads[5:]:
        copy.start()
    far[...] = jnp.zeros_like(far)

    barrier = pltpu.get_barrier_semaphore()
    partners = [sibling]
    for off in (1, 2, 3):
        partners += [at_xy(0, off), at_xy(1, off)]
    partners += [along_z(1), along_z(-1)]
    for partner in partners:
        pl.semaphore_signal(barrier, inc=1, device_id=partner, device_id_type=MESH)
    pl.semaphore_wait(barrier, len(partners))

    def tell(n):
        for off in (2**n, -(2**n)):
            pl.semaphore_signal(ready_sem.at[n], inc=1, device_id=along_z(off), device_id_type=MESH)

    def hear(n):
        pl.semaphore_wait(ready_sem.at[n], 2)

    def part_of(s, half, first, second, sub=None):
        rows = BLK // 2
        start = half * rows
        if sub is not None:
            start, rows = start + sub * (rows // 2), rows // 2
        at = (second, first) if half == 0 else (first, second)
        if s == 0:
            return kv.at[(*at, pl.ds(start, rows))]
        return qo.at[(*at, s - 1, pl.ds(start, rows))]

    rest = pl.ds(1, 3)

    def send(src, dst, send_to, received, device):
        pltpu.make_async_remote_copy(
            src_ref=src, dst_ref=dst, send_sem=send_to, recv_sem=received, device_id=device, device_id_type=MESH
        ).start()

    def wait(ref, sem):
        pltpu.make_async_copy(ref, ref, sem).wait()

    def around(s):
        return (2, 1, -1) if s == 2 else (1, -1)

    def start_first(s):
        for off in (1, -1, 2):
            for half in (0, 1):
                to = slot_of(-off)
                send(part_of(s, half, 0, 0), part_of(s, half, to, 0), send_sem.at[s], first_sem.at[s, half, to], at_xy(half, off))

    def start_second(s):
        for half in (0, 1):
            for off in around(s):
                to = slot_of(-off)
                send(part_of(s, half, 0, 0), part_of(s, half, 0, to), send_sem.at[s], second_sem.at[s, half, 0, to], at_xy(1 - half, off))

    def wait_first(s, half, first):
        wait(part_of(s, half, first, 0), first_sem.at[s, half, first])

    def pass_second(s, half, first, index):
        for off in around(s):
            to = slot_of(-off)
            send(
                part_of(s, half, first, 0), part_of(s, half, first, to), send_sem.at[s],
                second_sem.at[s, half, index, to], at_xy(1 - half, off),
            )

    def wait_second(s, half, first, index, second):
        wait(part_of(s, half, first, second), second_sem.at[s, half, index, second])

    def pass_third(s, half, first, index, second):
        sub = 0 if OFFSETS[second] == -1 else 1
        send(
            part_of(s, half, first, second, sub), part_of(s, half, first, 3, sub), send_sem.at[s],
            third_sem.at[s, half, index, sub], at_xy(1 - half, -OFFSETS[second]),
        )

    def wait_third(s, half, first, index):
        for sub in (0, 1):
            wait(part_of(s, half, first, 3, sub), third_sem.at[s, half, index, sub])

    def pass_seconds(s):
        for half in (0, 1):
            for first in (1, 2, 3):
                wait_first(s, half, first)
            pass_second(s, half, rest, 1)

    def pass_thirds(s):
        for half in (0, 1):
            for second in (1, 2):
                wait_second(s, half, 0, 0, second)
                wait_second(s, half, rest, 1, second)
                pass_third(s, half, pl.ds(0, 4), 0, second)

    def sent(s):
        rows = pl.ds(0, BLK * 15 // 16)
        wait(kv.at[:, :, rows] if s == 0 else qo.at[:, :, 0, rows], send_sem.at[s])

    def block_at(a, b):
        return mod4(y + OFFSETS[a]) * SIDE + mod4(x + OFFSETS[b])

    def project(weights, acc, slots, add):
        tokens = [x_buf[:, pl.ds(pl.multiple_of(block_at(a, b) * BLK, BLK), BLK)] for a, b in slots]
        term = jnp.dot(
            jnp.concatenate(tokens, axis=1), weights.reshape(len(slots) * BLK, weights.shape[-1]), preferred_element_type=F32
        )
        acc[...] = acc[...] + term if add else term

    loads[0].wait()
    loads[1].wait()
    start_first(0)
    start_second(0)
    tokens_out = pltpu.make_async_remote_copy(
        src_ref=tok_ref, dst_ref=own_tokens,
        send_sem=pair_send.at[0], recv_sem=pair_recv.at[0], device_id=sibling, device_id_type=MESH,
    )
    loads[4].start()
    tokens_out.start()
    tell(0)
    for first in (1, 2, 3):
        for half in (0, 1):
            wait_first(0, half, first)
            pass_second(0, half, first, first)
    hear(0)
    tell(1)
    loads[2].wait()
    loads[3].wait()
    start_first(1)
    for half in (0, 1):
        for second in (1, 2):
            wait_second(0, half, 0, 0, second)
            pass_third(0, half, 0, 0, second)
    start_second(1)
    for half in (0, 1):
        for second in (1, 2):
            for first in (1, 2, 3):
                wait_second(0, half, first, first, second)
            pass_third(0, half, rest, 1, second)
    hear(1)
    tell(2)
    pass_seconds(1)
    start_first(2)
    start_second(2)
    hear(2)
    loads[4].wait()
    loads[5].wait()
    tokens_out.wait()

    for a in range(3):
        project(kv[a, 0:3], kv_acc, [(a, b) for b in range(3)], a > 0)
    wait_third(0, 1, 0, 0)
    wait_third(0, 1, rest, 1)
    project(kv[0:3, 3], kv_acc, [(a, 3) for a in range(3)], True)
    wait_third(0, 0, 0, 0)
    wait_third(0, 0, rest, 1)
    project(kv[3], kv_acc, [(3, b) for b in range(4)], True)
    pass_thirds(1)
    keys_in = kv_acc[:, :HEAD]
    k_act[...] = (keys_in / (1.0 + jnp.exp(-keys_in))).astype(BF16)
    v_act[...] = kv_acc[:, HEAD:].astype(BF16)
    for b in (0, 1):
        rows = pl.ds(b * TOK, TOK)
        state[b] = lax.dot_general(
            k_act[rows], v_act[rows], (((0,), (0,)), ((), ())), preferred_element_type=F32
        )
    near[mem] = (state[0] + state[1]).astype(BF16)

    for off in (1, 2, 3):
        send(near.at[mem], near.at[mem], scan_send.at[off - 1], near_sem.at[mem], at_z(grp, mod4(mem + off)))
    pass_seconds(2)

    def send_wo(n, rows, columns):
        send(qo.at[rows, columns, 1], wo_pair.at[rows, columns], pair_send.at[1 + n], wo_recv.at[n], sibling)

    inner = pl.ds(0, 3)
    shares = [(inner, inner), (inner, 3), (3, pl.ds(0, 4))]
    for off in (1, 2, 3):
        m = mod4(mem + off)
        wait(near.at[m], near_sem.at[m])
    all_near = [near[m].astype(F32) for m in range(GROUP)]
    total[...] = (all_near[0] + all_near[1] + all_near[2] + all_near[3]).astype(BF16)

    targets = [(2, 3, 0), (2, 0, 3), (2, 3, 1), (2, 0, 2), (1, None, None), (3, None, None)]

    def sends_total(off, member):
        inside = grp + off < GROUPS
        return inside if member is None else jnp.logical_and(inside, mem == member)

    for n, (off, member, target) in enumerate(targets):

        @pl.when(sends_total(off, member))
        def _():
            pltpu.make_async_remote_copy(
                src_ref=total, dst_ref=far.at[grp], send_sem=scan_send.at[3 + n], recv_sem=far_sem.at[grp],
                device_id=at_z(grp + off, mem if target is None else target), device_id_type=MESH,
            ).start()

    prefix = jnp.zeros((HEAD, HEAD), F32)
    for m in range(GROUP - 1):
        prefix = prefix + jnp.where(m < mem, all_near[m], 0.0)

    for half in (0, 1):
        wait_third(1, half, pl.ds(0, 4), 0)
    for a in range(4):
        project(qo[a, :, 0], q_act, [(a, b) for b in range(4)], a > 0)
    queries = q_act[...]
    q_act[...] = queries / (1.0 + jnp.exp(-queries))
    causal = lax.broadcasted_iota(jnp.int32, (TOK, TOK), 0) >= lax.broadcasted_iota(jnp.int32, (TOK, TOK), 1)
    for b in (0, 1):
        rows = pl.ds(b * TOK, TOK)
        scores = lax.dot_general(
            q_act[rows].astype(BF16), k_act[rows], (((1,), (1,)), ((), ())), preferred_element_type=F32
        )
        scores = jnp.where(causal, scores, 0.0).astype(BF16)
        intra[rows] = jnp.dot(scores, v_act[rows], preferred_element_type=F32)
    for half in (0, 1):
        for second in (1, 2):
            wait_second(2, half, 0, 0, second)
            wait_second(2, half, rest, 1, second)
    send_wo(0, *shares[0])
    for g in range(GROUPS - 1):

        @pl.when(g < grp)
        def _():
            wait(far.at[g], far_sem.at[g])

        prefix = prefix + jnp.where(g < grp, far[g].astype(F32), 0.0)

    gain = gain_buf[pl.ds(core, 1), :]

    def normed(b):
        rows = pl.ds(pl.multiple_of(b * TOK, TOK), TOK)
        before = prefix + jnp.where(b == 1, state[0], 0.0)
        attended = intra[rows] + jnp.dot(
            q_act[rows].astype(BF16), before.astype(BF16), preferred_element_type=F32
        )
        meansq = jnp.mean(attended * attended, axis=-1, keepdims=True)
        return (attended * lax.rsqrt(meansq + 1e-06) * gain).astype(BF16)

    nrm_out[...] = normed(1 - core)
    nrm_copy = pltpu.make_async_remote_copy(
        src_ref=nrm_out, dst_ref=nrm.at[core], send_sem=pair_send.at[4], recv_sem=pair_recv.at[1],
        device_id=sibling, device_id_type=MESH,
    )
    nrm_copy.start()
    nrm[core] = normed(core)
    for half in (0, 1):
        wait_second(2, half, 0, 0, 3)
        wait_second(2, half, rest, 1, 3)
    for n in (1, 2):
        send_wo(n, *shares[n])
    nrm_copy.wait()
    lhs = jnp.concatenate([nrm[0], nrm[1]], axis=1)
    order = [(a, b) for a in range(3) for b in range(3)] + [(a, 3) for a in range(3)] + [(3, b) for b in range(4)]
    for n, (a, b) in enumerate(order):
        if n in (0, 9, 12):
            share = (0, 9, 12).index(n)
            wait(wo_pair.at[shares[share]], wo_recv.at[share])
        block = block_at(a, b)
        columns = pl.ds(pl.multiple_of(block * BLK, BLK), BLK)
        own, other = qo[a, b, 1], wo_pair[a, b]
        weights = jnp.concatenate([jnp.where(core == 0, own, other), jnp.where(core == 0, other, own)], axis=1)
        out_ref[:, columns] = jnp.dot(lhs, weights, preferred_element_type=F32).astype(BF16)
    for s in range(3):
        sent(s)
    for off in (1, 2, 3):
        wait(near.at[0], scan_send.at[off - 1])
    for n, share in enumerate(shares):
        wait(wo_pair.at[share], pair_send.at[1 + n])
    for n, (off, member, _) in enumerate(targets):

        @pl.when(sends_total(off, member))
        def _():
            wait(total, scan_send.at[3 + n])


def shards(tokens, w_qkv, norm_gain, w_out):
    hbm = pl.BlockSpec(memory_space=pl.ANY)
    dma = pltpu.SemaphoreType.DMA
    width = tokens.shape[2]
    out = pl.pallas_call(
        kernel,
        out_shape=jax.ShapeDtypeStruct((TOK, width), BF16),
        in_specs=[hbm] * 4,
        out_specs=pl.BlockSpec(memory_space=pltpu.VMEM),
        scratch_shapes=[
            pltpu.VMEM((2 * TOK, width), BF16),
            pltpu.VMEM((SIDE, SIDE, BLK, 2 * HEAD), BF16),
            pltpu.VMEM((SIDE, SIDE, 2, BLK, HEAD), BF16),
            pltpu.VMEM((SIDE, SIDE, BLK, HEAD), BF16),
            pltpu.VMEM((2 * TOK, HEAD), BF16),
            pltpu.VMEM((2 * TOK, HEAD), BF16),
            pltpu.VMEM((2 * TOK, HEAD), F32),
            pltpu.VMEM((GROUP, HEAD, HEAD), BF16),
            pltpu.VMEM((GROUPS, HEAD, HEAD), BF16),
            pltpu.VMEM((HEAD, HEAD), BF16),
            pltpu.VMEM((2, TOK, HEAD), BF16),
            pltpu.VMEM((TOK, HEAD), BF16),
            pltpu.VMEM((2, HEAD), F32),
            pltpu.VMEM((2 * TOK, 2 * HEAD), F32),
            pltpu.VMEM((2 * TOK, HEAD), F32),
            pltpu.VMEM((2, HEAD, HEAD), F32),
            dma((6,)),
            dma((3,)),
            dma((3, 2, 4)),
            dma((3, 2, 4, 4)),
            dma((3, 2, 2, 2)),
            dma((9,)),
            dma((GROUP,)),
            dma((GROUPS,)),
            dma((5,)),
            dma((2,)),
            dma((3,)),
            pltpu.SemaphoreType.REGULAR((3,)),
        ],
        compiler_params=pltpu.CompilerParams(
            collective_id=0, has_side_effects=True, vmem_limit_bytes=48 * 1024 * 1024
        ),
        name="attention_layer",
    )(*(pltpu.with_memory_space_constraint(a, pltpu.HBM) for a in (tokens[0], w_qkv, norm_gain.reshape(2, HEAD), w_out)))
    return out[None]


def solution(mesh):
    return jax.shard_map(
        shards,
        mesh=mesh,
        in_specs=(P("dp", "seq", None), P("dp", None), P(), P(None, "dp")),
        out_specs=P("dp", "seq", None),
        check_vma=False,
    )
```
